32 devices in a mesh: group: 8 (over z, core), dev: 4 (over y, x).
Axes of the slice: x: 2, y: 2, z: 4, core: 2. Of those that a mesh axis runs over, the one named last changes fastest.
Arguments:
- tiles: bfloat16 [2304, 5, 128, 128], P(('group', 'dev')), may hold values from 0.00029945374 to 0.029907227
- tile_col: int32 [2304, 5], P(('group', 'dev')), may hold values from 0 to 15
- strip_group: int32 [2304], P(('group', 'dev')), may hold values from 0 to 7, as said below
- strip_slot: int32 [2304], P(('group', 'dev')), may hold values from 0 to 15
- live_count: int32 [32], P(('group', 'dev')), may hold values from 36 to 72, as said below
- omega: bfloat16 [16384, 128], P(('group', 'dev')), may hold values from -40 to 40
- idf: float32 [65536], P(('group', 'dev')), may hold values from 0.4 to 20
Outputs:
- q_basis: float32 [65536, 128], P(('group', 'dev'))
- doc_factor: bfloat16 [128, 16384], P(None, ('group', 'dev'))
The draws below stay inside these ranges and needn't reach their ends.
Inputs may be any that keep to these rules, and one draw needn't show every extreme that they name: `strip_group`: among the 72 strips of one device at most 12 name one group; in every draw one group is named by exactly 12 strips of every device. `live_count`: some device has all 72 strips live.
All inputs are finite; a program needn't handle non-finite values.
Results may differ from the reference program's by a relative error of at most 0.0034.
Values may be sent and summed in bfloat16 or wider, within the bound.
No kernel may reach another device: no remote copies, remote signals or barrier semaphores. Data moves between devices by JAX's collectives and lax.ppermute only.
A program may use at most 128 MiB of HBM per device.

```python
import math
import jax
import jax.numpy as jnp
from jax import lax

TILE = 128
SKETCH = 128
RB_DEV = 16
RT = 72
TPI = 5
CAP = 12
CB_G = 16
STRIPS = 2304
TERMS = 65536
DOCS = 16384
N_GROUP = 8
N_DEV = 4
DEVICES = 32


def draw_strip_group(key, part):
    base = jax.random.fold_in(key, 11)
    full_group = jax.random.randint(jax.random.fold_in(base, 1), (), 0, N_GROUP)
    device_keys = jax.random.split(jax.random.fold_in(base, 2), DEVICES)

    def one_device(device_key):
        seat_key, order_key = jax.random.split(device_key)
        seats = jnp.arange((N_GROUP - 1) * CAP, dtype=jnp.int32) // CAP
        seats = jax.random.permutation(seat_key, seats)[:RT - CAP]
        others = seats + (seats >= full_group).astype(jnp.int32)
        labels = jnp.concatenate([jnp.zeros((CAP,), jnp.int32) + full_group, others])
        return jax.random.permutation(order_key, labels)
    return jax.vmap(one_device)(device_keys).reshape(DEVICES * RT).astype(jnp.int32)


def draw_live_count(key, part):
    base = jax.random.fold_in(key, 23)
    counts = jax.random.randint(jax.random.fold_in(base, 1), (DEVICES,), RT // 2, RT + 1)
    busiest = jax.random.randint(jax.random.fold_in(base, 2), (), 0, DEVICES)
    return jnp.where(jnp.arange(DEVICES) == busiest, RT, counts).astype(jnp.int32)


def draw_omega(key, part):
    base = jax.random.fold_in(key, 41)
    col_key, value_key = jax.random.split(base)
    scales = jnp.exp(jax.random.uniform(col_key, (SKETCH,), jnp.float32, 0.0, math.log(10.0)))
    values = jnp.clip(jax.random.normal(value_key, (DOCS, SKETCH), jnp.float32), -4.0, 4.0)
    return (values * scales[None, :]).astype(jnp.bfloat16)


def draw_idf(key, part):
    base = jax.random.fold_in(key, 37)
    position = jnp.arange(TERMS, dtype=jnp.float32) / TERMS
    rough = jnp.exp(jax.random.uniform(base, (TERMS,), jnp.float32, math.log(0.5), math.log(2.0)))
    return (1.0 + 3.0 * position) * rough


def touch_ends(array, stream_key, low, high):
    spot = [jax.random.randint(jax.random.fold_in(stream_key, axis), (), 0, length) for axis, length in enumerate(array.shape)]
    longest = array.shape.index(max(array.shape))
    next_to = spot[:longest] + [(spot[longest] + 1) % array.shape[longest]] + spot[longest + 1:]
    return array.at[tuple(spot)].set(low).at[tuple(next_to)].set(high)


def shard_levels(key, extent, cuts, least, top_value):
    level = 1.0
    for dim, shards_of in cuts:
        steps = jax.random.uniform(jax.random.fold_in(jax.random.fold_in(key, 6), dim), (shards_of,), jnp.float32, least / len(cuts), top_value / len(cuts))
        level = level * jnp.repeat(jnp.exp(steps), extent[dim] // shards_of).reshape((-1,) + (1,) * (len(extent) - 1 - dim))
    return level


def setup_inputs(seed: int = 0) -> dict:
    keys = jax.random.split(jax.random.key(seed), 8)
    return {
        "tiles": jnp.clip(jnp.exp(math.log(0.029907227) - 4.6038955 * jax.random.uniform(keys[0], (STRIPS, TPI, TILE, TILE), jnp.float32) ** shard_levels(keys[0], (STRIPS, TPI, TILE, TILE), ((0, 32),), -0.2, 0.2)), 0.00029945374, 0.029907227).astype(jnp.bfloat16),
        "tile_col": touch_ends(jax.random.randint(keys[1], (STRIPS, TPI), 0, CB_G), jax.random.fold_in(keys[1], 1), 0, CB_G - 1).astype(jnp.int32),
        "strip_group": draw_strip_group(jax.random.fold_in(keys[7], 71), 0),
        "strip_slot": touch_ends(jax.random.randint(keys[3], (STRIPS,), 0, RB_DEV), jax.random.fold_in(keys[3], 1), 0, RB_DEV - 1).astype(jnp.int32),
        "live_count": draw_live_count(jax.random.fold_in(keys[7], 71), 0),
        "omega": draw_omega(jax.random.fold_in(keys[7], 71), 0),
        "idf": draw_idf(jax.random.fold_in(keys[7], 71), 0),
    }


def reference(tiles, tile_col, strip_group, strip_slot, live_count, omega, idf):
    n_devices = N_GROUP * N_DEV
    strip_index = jnp.arange(STRIPS, dtype=jnp.int32)
    holder = strip_index // RT
    band_index = holder % N_DEV
    group_index = holder // N_DEV
    live_mask = (strip_index % RT < live_count[holder]).astype(jnp.float32)
    block_row = ((strip_group * N_DEV + band_index) * RB_DEV + strip_slot).astype(jnp.int32)
    block_col = (group_index[:, None] * CB_G + tile_col).astype(jnp.int32)
    omega_blocks = omega.reshape(DOCS // TILE, TILE, SKETCH)

    def strip_terms(inputs):
        tile_set, col_ids, alive_mask = inputs
        picked = omega_blocks[col_ids].astype(jnp.float32)
        product = jnp.einsum('stij,stjk->sik', tile_set.astype(jnp.float32), picked)
        return product * alive_mask[:, None, None]
    partial_value = lax.map(strip_terms, (tiles.reshape(n_devices, RT, TPI, TILE, TILE), block_col.reshape(n_devices, RT, TPI), live_mask.reshape(n_devices, RT)))
    partial_value = partial_value.reshape(STRIPS, TILE, SKETCH)
    summed = jax.ops.segment_sum(partial_value, block_row, num_segments=TERMS // TILE)
    sketch = summed.reshape(TERMS, SKETCH) * idf[:, None]
    gram_matrix = lax.dot_general(sketch.astype(jnp.float32), sketch.astype(jnp.float32), (((0,), (0,)), ((), ())), precision=lax.Precision.HIGHEST, preferred_element_type=jnp.float32) / TERMS
    lower_factor = jnp.linalg.cholesky(gram_matrix)
    q_basis = jax.scipy.linalg.solve_triangular(lower_factor, sketch.T, lower=True).T
    weighted = (idf[:, None] * q_basis).astype(jnp.bfloat16)
    weighted_blocks = weighted.reshape(TERMS // TILE, TILE, SKETCH)

    def doc_terms(running, inputs):
        tile_set, col_ids, row_ids, alive_mask = inputs
        q_rows = weighted_blocks[row_ids].astype(jnp.float32) * alive_mask[:, None, None]
        contrib = jnp.einsum('sik,stij->stkj', q_rows, tile_set.astype(jnp.float32))
        running = running.at[col_ids.reshape(-1)].add(contrib.reshape(-1, SKETCH, TILE))
        return (running, None)
    initial = jnp.zeros((DOCS // TILE, SKETCH, TILE), jnp.float32)
    running, unused = lax.scan(doc_terms, initial, (tiles.reshape(n_devices, RT, TPI, TILE, TILE), block_col.reshape(n_devices, RT, TPI), block_row.reshape(n_devices, RT), live_mask.reshape(n_devices, RT)))
    doc_factor = jnp.transpose(running, (1, 0, 2)).reshape(SKETCH, DOCS).astype(jnp.bfloat16)
    return (q_basis, doc_factor)
```

```python
import functools
import jax
import jax.numpy as jnp
from jax import lax
from jax.experimental import pallas as pl
from jax.experimental.pallas import tpu as pltpu
from jax.sharding import PartitionSpec as P

F32 = jnp.float32
BF16 = jnp.bfloat16
HIGHEST = lax.Precision.HIGHEST


def strips_per_step(strips, most=8):
    return max(s for s in range(1, most + 1) if strips % s == 0)


def sketch_kernel(owned, step_strips, group_ref, slot_ref, col_ref, live_ref, place_ref,
                  tiles_ref, omega_ref, mine_ref, theirs_ref, acc_ref, out_ref, sems):
    step = pl.program_id(0)
    tpi = tiles_ref.shape[1]
    half = mine_ref.shape[0]
    core = place_ref[0] % 2

    @pl.when(step == 0)
    def _():
        acc_ref[...] = jnp.zeros_like(acc_ref)

    for i in range(step_strips):
        strip = step * step_strips + i

        @pl.when(strip < live_ref[0])
        def _():
            owner = group_ref[strip]
            side = jnp.where(owner % 2 == core, 0, 1)
            block = side * half + (owner // 2) * owned + slot_ref[strip]
            left = jnp.concatenate([tiles_ref[i, j] for j in range(tpi)], axis=1)
            right = jnp.concatenate([omega_ref[col_ref[strip, j]] for j in range(tpi)], axis=0)
            acc_ref[block] += jnp.dot(left, right, preferred_element_type=F32)

    @pl.when(step == pl.num_programs(0) - 1)
    def _():
        keep = pltpu.make_async_copy(acc_ref.at[pl.ds(0, half)], mine_ref, sems.at[0])
        keep.start()
        out_ref[...] = acc_ref[pl.ds(half, half)].astype(BF16)
        give = pltpu.make_async_copy(out_ref, theirs_ref, sems.at[1])
        give.start()
        keep.wait()
        give.wait()


def partial_sketch(group, slot, col, live, place, tiles, omega_blocks, n_group, owned):
    strips, tpi, edge, _ = tiles.shape
    cols = omega_blocks.shape[-1]
    per = strips_per_step(strips)
    half = n_group // 2 * owned
    return pl.pallas_call(
        functools.partial(sketch_kernel, owned, per),
        out_shape=(
            jax.ShapeDtypeStruct((half, edge, cols), F32),
            jax.ShapeDtypeStruct((half, edge, cols), BF16),
        ),
        grid_spec=pltpu.PrefetchScalarGridSpec(
            num_scalar_prefetch=5,
            grid=(strips // per,),
            in_specs=[
                pl.BlockSpec((per, tpi, edge, edge), lambda s, *_: (s, 0, 0, 0)),
                pl.BlockSpec(omega_blocks.shape, lambda s, *_: (0, 0, 0)),
            ],
            out_specs=(pl.BlockSpec(memory_space=pl.ANY), pl.BlockSpec(memory_space=pl.ANY)),
            scratch_shapes=[
                pltpu.VMEM((2 * half, edge, cols), F32),
                pltpu.VMEM((half, edge, cols), BF16),
                pltpu.SemaphoreType.DMA((2,)),
            ],
        ),
        name="partial_sketch",
    )(group, slot, col, live, place, tiles, omega_blocks)


def combine_kernel(place_ref, mine_ref, pair_ref, up_ref, down_ref, idf_ref,
                   sketch_ref, weight_ref, gram_ref):
    step = pl.program_id(0)
    blocks = sketch_ref.shape[0]
    total = mine_ref[0] + pair_ref[0].astype(F32) + up_ref[...].astype(F32) + down_ref[...].astype(F32)
    gram = jnp.zeros(gram_ref.shape, F32)
    for b in range(blocks):
        row = idf_ref[b]
        scale = jnp.transpose(jnp.broadcast_to(row, (total.shape[2], total.shape[1])))
        sk = total[b] * scale
        sketch_ref[b] = sk
        weight_ref[b] = jnp.transpose(sk * scale).astype(BF16)
        gram += lax.dot_general(sk, sk, (((0,), (0,)), ((), ())), precision=HIGHEST,
                                preferred_element_type=F32)

    @pl.when(step == 0)
    def _():
        gram_ref[...] = gram

    @pl.when(step > 0)
    def _():
        gram_ref[...] += gram


def combine(place, mine, pair, up, down, idf):
    chips, owned, edge, cols = mine.shape
    per = max(s for s in (1, 2, 4) if owned % s == 0)
    part = pl.BlockSpec((1, per, edge, cols), lambda s, place: (place[0] // 2, s, 0, 0))
    plain = pl.BlockSpec((per, edge, cols), lambda s, place: (s, 0, 0))
    return pl.pallas_call(
        combine_kernel,
        out_shape=(
            jax.ShapeDtypeStruct((owned, edge, cols), F32),
            jax.ShapeDtypeStruct((owned, cols, edge), BF16),
            jax.ShapeDtypeStruct((cols, cols), F32),
        ),
        grid_spec=pltpu.PrefetchScalarGridSpec(
            num_scalar_prefetch=1,
            grid=(owned // per,),
            in_specs=[part, part, plain, plain,
                      pl.BlockSpec((per, 1, edge), lambda s, place: (s, 0, 0))],
            out_specs=(plain, pl.BlockSpec((per, cols, edge), lambda s, place: (s, 0, 0)),
                       pl.BlockSpec((cols, cols), lambda s, place: (0, 0))),
        ),
        name="combine",
    )(place, mine, pair, up, down, idf.reshape(owned, 1, edge))


def project_kernel(owned, step_strips, chips, group_ref, slot_ref, col_ref, live_ref, place_ref,
                   tiles_ref, *rest):
    n_src = 2 + 4 * (chips - 1)
    sources = rest[:n_src]
    doc_ref, weights_ref, sems = rest[n_src:]
    step = pl.program_id(0)
    tpi, edge = tiles_ref.shape[1], tiles_ref.shape[3]
    chip, core = place_ref[0] // 2, place_ref[0] % 2

    away = [(0, 0), (0, 1)]
    for t in range(1, chips):
        away += [(-t, 0), (-t, 1), (t, 0), (t, 1)]

    @pl.when(step == 0)
    def _():
        doc_ref[...] = jnp.zeros_like(doc_ref)
        for wait in (False, True):
            for n, (far, other) in enumerate(away):
                there = chip + far

                @pl.when((there >= 0) & (there < chips))
                def _():
                    owner = there * 2 + (core if other == 0 else 1 - core)
                    copy = pltpu.make_async_copy(
                        sources[n], weights_ref.at[pl.ds(owner * owned, owned)], sems.at[n])
                    copy.wait() if wait else copy.start()

    for i in range(step_strips):
        strip = step * step_strips + i

        @pl.when(strip < live_ref[0])
        def _():
            left = weights_ref[group_ref[strip] * owned + slot_ref[strip]]
            right = jnp.concatenate([tiles_ref[i, j] for j in range(tpi)], axis=1)
            out = jnp.dot(left, right, preferred_element_type=F32)
            for j in range(tpi):
                doc_ref[col_ref[strip, j]] += out[:, j * edge:(j + 1) * edge]


def project(group, slot, col, live, place, tiles, sources, n_group, owned, col_blocks):
    strips, tpi, edge, _ = tiles.shape
    cols = sources[0].shape[1]
    per = strips_per_step(strips)
    chips = n_group // 2
    return pl.pallas_call(
        functools.partial(project_kernel, owned, per, chips),
        out_shape=jax.ShapeDtypeStruct((col_blocks, cols, edge), F32),
        grid_spec=pltpu.PrefetchScalarGridSpec(
            num_scalar_prefetch=5,
            grid=(strips // per,),
            in_specs=[pl.BlockSpec((per, tpi, edge, edge), lambda s, *_: (s, 0, 0, 0))]
            + [pl.BlockSpec(memory_space=pl.ANY)] * len(sources),
            out_specs=pl.BlockSpec((col_blocks, cols, edge), lambda s, *_: (0, 0, 0)),
            scratch_shapes=[
                pltpu.VMEM((n_group * owned, cols, edge), BF16),
                pltpu.SemaphoreType.DMA((len(sources),)),
            ],
        ),
        name="project",
    )(group, slot, col, live, place, tiles, *sources)


def finish_kernel(place_ref, own_ref, inverse_ref, *rest):
    arrived, out_ref = rest[:-1], rest[-1]
    blocks, _, edge = own_ref.shape[1:]
    for b in range(blocks):
        total = own_ref[0, b]
        for r in arrived:
            total += r[b].astype(F32)
        out_ref[:, b * edge:(b + 1) * edge] = jnp.dot(
            inverse_ref[...], total, precision=HIGHEST, preferred_element_type=F32).astype(BF16)


def finish(place, own, inverse, arrived):
    n_dev, blocks, cols, edge = own.shape
    return pl.pallas_call(
        finish_kernel,
        out_shape=jax.ShapeDtypeStruct((cols, blocks * edge), BF16),
        grid_spec=pltpu.PrefetchScalarGridSpec(
            num_scalar_prefetch=1,
            grid=(1,),
            in_specs=[pl.BlockSpec((1, blocks, cols, edge), lambda s, place: (place[1], 0, 0, 0)),
                      pl.BlockSpec((cols, cols), lambda s, place: (0, 0))]
            + [pl.BlockSpec((blocks, cols, edge), lambda s, place: (0, 0, 0))] * len(arrived),
            out_specs=pl.BlockSpec((cols, blocks * edge), lambda s, place: (0, 0)),
        ),
        name="finish",
    )(place, own, inverse, *arrived)


def partners(n, s):
    if n & (n - 1) == 0:
        return [(i, i ^ s) for i in range(n)]
    return [(i, (i + s) % n) for i in range(n)]


def partner_of(n, me, s):
    return me ^ s if n & (n - 1) == 0 else (me + s) % n


def sum_over(x, axis, n):
    if n & (n - 1):
        return lax.psum(x, axis)
    s = 1
    while s < n:
        x = x + lax.ppermute(x, axis, partners(n, s))
        s *= 2
    return x


def on_device(tiles, tile_col, strip_group, strip_slot, live_count, omega, idf):
    n_group = lax.axis_size("group")
    n_dev = lax.axis_size("dev")
    chips = n_group // 2
    edge = tiles.shape[2]
    cols = omega.shape[1]
    owned = idf.shape[0] // edge
    me, band = lax.axis_index("group"), lax.axis_index("dev")
    chip = me // 2
    place = jnp.stack([me, band]).astype(jnp.int32)

    col_own = omega.shape[0] // edge
    own_omega = omega.reshape(col_own, edge, cols)
    group_omega = jnp.zeros((n_dev,) + own_omega.shape, BF16)
    group_omega = lax.dynamic_update_slice(group_omega, own_omega[None], (band, 0, 0, 0))
    for s in range(1, n_dev):
        sent = lax.ppermute(own_omega, "dev", partners(n_dev, s))
        source = partner_of(n_dev, band, s if n_dev & (n_dev - 1) == 0 else n_dev - s)
        group_omega = lax.dynamic_update_slice(group_omega, sent[None], (source, 0, 0, 0))
    omega_blocks = group_omega.reshape(n_dev * col_own, edge, cols)

    mine, theirs = partial_sketch(strip_group, strip_slot, tile_col, live_count, place,
                                  tiles, omega_blocks, n_group, owned)
    pair = lax.ppermute(theirs, "group", [(i, i ^ 1) for i in range(n_group)])
    mine = mine.reshape(chips, owned, edge, cols)
    pair = pair.reshape(chips, owned, edge, cols)

    up = jnp.zeros((owned, edge, cols), BF16)
    down = up
    for t in range(1, chips):
        up_unit = jnp.clip(chips - t + chip, 0, chips - 1)
        down_unit = jnp.clip(t - chips + chip, 0, chips - 1)

        def outgoing(unit, carried):
            total = (lax.dynamic_index_in_dim(mine, unit, 0, False)
                     + lax.dynamic_index_in_dim(pair, unit, 0, False).astype(F32))
            if t > 1:
                total = total + carried.astype(F32)
            return total.astype(BF16)

        to_up, to_down = outgoing(up_unit, up), outgoing(down_unit, down)
        up_links = [(c, c + 1) for c in range(min(t, chips - 1))]
        down_links = [(chips - 1 - a, chips - 1 - b) for a, b in up_links]
        both = lambda links: [(2 * a + k, 2 * b + k) for a, b in links for k in (0, 1)]
        up = lax.ppermute(to_up, "group", both(up_links))
        down = lax.ppermute(to_down, "group", both(down_links))

    sketch, weight, local_gram = combine(place, mine, pair, up, down, idf)

    swap = lambda x: lax.ppermute(x, "group", [(i, i ^ 1) for i in range(n_group)])
    sources = [weight, swap(weight)]
    below = above = weight
    for t in range(1, chips):
        below = lax.ppermute(below, "group", [(i, i + 2) for i in range(n_group - 2)])
        above = lax.ppermute(above, "group", [(i + 2, i) for i in range(n_group - 2)])
        sources += [below, swap(below), above, swap(above)]

    gram_matrix = sum_over(sum_over(local_gram, "dev", n_dev), "group", n_group)
    gram_matrix = gram_matrix / (idf.shape[0] * n_group * n_dev)
    lower_factor = jnp.linalg.cholesky(gram_matrix)
    inverse = jax.scipy.linalg.solve_triangular(lower_factor, jnp.eye(cols, dtype=F32), lower=True)
    q_basis = lax.dot_general(sketch.reshape(-1, cols), inverse, (((1,), (1,)), ((), ())),
                              precision=HIGHEST, preferred_element_type=F32)

    doc_part = project(strip_group, strip_slot, tile_col, live_count, place, tiles, sources,
                       n_group, owned, n_dev * col_own)
    doc_part = doc_part.reshape(n_dev, col_own, cols, edge)
    arrived = []
    for s in range(1, n_dev):
        unit = lax.dynamic_index_in_dim(doc_part, partner_of(n_dev, band, s), 0, False)
        arrived.append(lax.ppermute(unit.astype(BF16), "dev", partners(n_dev, s)))
    doc_factor = finish(place, doc_part, inverse, arrived)
    return (q_basis, doc_factor)


def solution(mesh):
    placed = (
        P(("group", "dev"), None, None, None),
        P(("group", "dev"), None),
        P(("group", "dev")),
        P(("group", "dev")),
        P(("group", "dev")),
        P(("group", "dev"), None),
        P(("group", "dev")),
    )
    return jax.shard_map(
        on_device,
        mesh=mesh,
        in_specs=placed,
        out_specs=(P(("group", "dev"), None), P(None, ("group", "dev"))),
        check_vma=False,
    )
```

```python
import functools
import jax
import jax.numpy as jnp
from jax import lax
from jax.experimental import pallas as pl
from jax.experimental.pallas import tpu as pltpu
from jax.sharding import PartitionSpec as P

F32 = jnp.float32
BF16 = jnp.bfloat16
HIGHEST = lax.Precision.HIGHEST
BATCH = 4

VM = pl.BlockSpec(memory_space=pltpu.VMEM)
SM = pl.BlockSpec(memory_space=pltpu.SMEM)
HB = pl.BlockSpec(memory_space=pltpu.HBM)


def near(x):
    return pltpu.with_memory_space_constraint(x, pltpu.VMEM)


def far_off(x):
    return pltpu.with_memory_space_constraint(x, pltpu.HBM)


def cost(strips):
    return pl.CostEstimate(flops=strips << 28, bytes_accessed=strips << 19, transcendentals=0)


def params(mib):
    return pltpu.CompilerParams(vmem_limit_bytes=mib << 20)


def far_chip(chip, chips):
    return jnp.where(chip < chips // 2, chips - 1, 0)


def collect(keep, group_ref, live_ref, list_ref, tiles_ref, buf_ref, sems):
    def scan(strip, count):
        hit = keep(group_ref[strip])

        @pl.when(hit)
        def _():
            list_ref[count] = strip
            pltpu.make_async_copy(tiles_ref.at[strip], buf_ref.at[count], sems.at[count]).start()

        return count + hit.astype(jnp.int32)

    return lax.fori_loop(0, live_ref[0], scan, jnp.int32(0))


def in_batches(count, list_ref, tiles_ref, buf_ref, sems, work):
    def trip(b, carry):
        for i in range(BATCH):
            at = b * BATCH + i

            @pl.when(at < count)
            def _():
                pltpu.make_async_copy(tiles_ref.at[0], buf_ref.at[at], sems.at[at]).wait()

        for i in range(BATCH):
            at = jnp.minimum(b * BATCH + i, count - 1)
            work(list_ref[at], at, (b * BATCH + i < count).astype(F32))
        return carry

    lax.fori_loop(0, (count + BATCH - 1) // BATCH, trip, jnp.int32(0))


def sketch_kernel(far_only, chips, owned, n_src, group_ref, slot_ref, col_ref, live_ref, place_ref,
                  tiles_ref, *rest):
    sources = rest[:n_src]
    both_ref, theirs_ref, omega_ref, list_ref, buf_ref, sems = rest[-6:]
    half = theirs_ref.shape[0]
    tpi = buf_ref.shape[1]
    strips = buf_ref.shape[0]
    me, band = place_ref[0], place_ref[1]
    chip, core = me // 2, me % 2
    far = far_chip(chip, chips)
    held = sources[0].shape[0]
    own = pltpu.make_async_copy(sources[0], omega_ref.at[pl.ds(band * held, held)],
                                sems.at[strips])
    own.start()
    count = collect(lambda g: (g // 2 == far) == far_only, group_ref, live_ref, list_ref,
                    tiles_ref, buf_ref, sems)
    both_ref[...] = jnp.zeros_like(both_ref)
    for s in range(1, n_src):
        omega_ref[pl.ds(partner_of(n_src, band, s, back=True) * held, held)] = sources[s][...]
    own.wait()

    def work(strip, at, valid):
        owner = group_ref[strip]
        unit = jnp.int32(0) if far_only else owner // 2 - (far == 0).astype(jnp.int32)
        side = jnp.where(owner % 2 == core, 0, half)
        block = side + unit * owned + slot_ref[strip]
        left = jnp.concatenate([buf_ref[at, j] for j in range(tpi)], axis=1)
        right = jnp.concatenate([omega_ref[col_ref[strip, j]] for j in range(tpi)], axis=0)
        both_ref[block] += jnp.dot(left, right, preferred_element_type=F32) * valid

    in_batches(count, list_ref, tiles_ref, buf_ref, sems, work)
    theirs_ref[...] = both_ref[pl.ds(half, half)].astype(BF16)


def partial_sketch(far_only, scalars, tiles, sources, chips, owned, after=()):
    strips, tpi, edge, _ = tiles.shape
    col_own, _, cols = sources[0].shape
    blocks = owned * (1 if far_only else chips - 1)
    return pl.pallas_call(
        functools.partial(sketch_kernel, far_only, chips, owned, len(sources)),
        out_shape=(pltpu.VMEM((2 * blocks, edge, cols), F32),
                   pltpu.VMEM((blocks, edge, cols), BF16)),
        in_specs=[SM] * 5 + [HB] * 2 + [VM] * (len(sources) - 1 + len(after)),
        out_specs=(VM, VM),
        scratch_shapes=[
            pltpu.VMEM((col_own * len(sources), edge, cols), BF16),
            pltpu.SMEM((strips,), jnp.int32),
            pltpu.VMEM((strips, tpi, edge, edge), BF16),
            pltpu.SemaphoreType.DMA((strips + 1,)),
        ],
        compiler_params=params(16),
        cost_estimate=cost(strips // 4 if far_only else strips),
        name="sketch_far" if far_only else "sketch_rest",
    )(*scalars, far_off(tiles), far_off(sources[0]), *[near(s) for s in (*sources[1:], *after)])


def first_kernel(blocks, piece, mine_ref, pair_ref, out_ref):
    rows = pl.ds(piece * blocks, blocks)
    out_ref[...] = (mine_ref[rows] + pair_ref[rows].astype(F32)).astype(BF16)


def relay_kernel(t, chips, owned, blocks, piece, place_ref, far_mine, far_pair, rest_mine,
                 rest_pair, up_ref, down_ref, to_up, to_down):
    chip = place_ref[0] // 2
    far = far_chip(chip, chips)
    for unit, carried, out in ((chips - t + chip, up_ref, to_up),
                               (t - chips + chip, down_ref, to_down)):
        unit = jnp.clip(unit, 0, chips - 1)

        @pl.when(unit == far)
        def _():
            rows = pl.ds(piece * blocks, blocks)
            out[...] = (far_mine[rows] + far_pair[rows].astype(F32)
                        + carried[...].astype(F32)).astype(BF16)

        @pl.when(unit != far)
        def _():
            unit_at = unit - (far == 0).astype(jnp.int32)
            rows = pl.ds(unit_at * owned + piece * blocks, blocks)
            out[...] = (rest_mine[rows] + rest_pair[rows].astype(F32)
                        + carried[...].astype(F32)).astype(BF16)


def combine_kernel(chips, owned, piece, place_ref, rest_mine, rest_pair, up_ref, down_ref,
                   idf_ref, gram_in, sketch_ref, weight_ref, gram_ref):
    blocks = sketch_ref.shape[0]
    chip = place_ref[0] // 2
    unit_at = chip - (far_chip(chip, chips) == 0).astype(jnp.int32)
    gram = gram_in[...]
    for b in range(blocks):
        at = unit_at * owned + piece * blocks + b
        total = (rest_mine[at] + rest_pair[at].astype(F32)
                 + up_ref[b].astype(F32) + down_ref[b].astype(F32))
        row = idf_ref[pl.ds(piece * blocks + b, 1), :]
        scale = jnp.transpose(jnp.broadcast_to(row, total.shape[::-1]))
        sk = total * scale
        sketch_ref[b] = sk
        weight_ref[b] = jnp.transpose(sk * scale).astype(BF16)
        gram += lax.dot_general(sk, sk, (((0,), (0,)), ((), ())), precision=HIGHEST,
                                preferred_element_type=F32)
    gram_ref[...] = gram


def factor_kernel(total_terms, gram_ref, inverse_ref, x_ref):
    n = gram_ref.shape[0]
    x_ref[...] = gram_ref[...] * (1.0 / total_terms)
    rows = lax.broadcasted_iota(jnp.int32, (n, n), 0)
    columns = lax.broadcasted_iota(jnp.int32, (n, n), 1)

    one_row = lax.broadcasted_iota(jnp.int32, (1, n), 1)

    def eliminate(j, carry):
        x = x_ref[...]
        row = x_ref[pl.ds(j, 1), :]
        column = jnp.take_along_axis(x, jnp.full((n, n), j, jnp.int32), axis=1)
        pivot = jnp.take_along_axis(jnp.broadcast_to(row, (8, n)),
                                    jnp.full((8, n), j, jnp.int32), axis=1)[:1]
        scaled = jnp.where(one_row == j, 1.0, row) / pivot
        below = rows > j
        x = jnp.where((columns == j) & below, 0.0, x)
        x_ref[...] = x - jnp.where(below, column, 0.0) * scaled
        return carry

    lax.fori_loop(0, n, eliminate, jnp.int32(0))
    x = x_ref[...]
    pivots = jnp.sum(jnp.where(rows == columns, x, 0.0), axis=1, keepdims=True)
    lower = jnp.where(rows > columns, x, jnp.where(rows == columns, 1.0, 0.0))
    inverse_ref[...] = lower * lax.rsqrt(pivots)


def basis_kernel(inverse_ref, *rest):
    pieces, q_ref = rest[:-1], rest[-1]
    at = 0
    for piece in pieces:
        for b in range(piece.shape[0]):
            q_ref[at] = lax.dot_general(piece[b], inverse_ref[...], (((1,), (1,)), ((), ())),
                                        precision=HIGHEST, preferred_element_type=F32)
            at += 1


def project_kernel(last, chips, owned, away, group_ref, slot_ref, col_ref, live_ref, place_ref,
                   tiles_ref, *rest):
    n_src = len(away)
    sources, rest = rest[:n_src], rest[n_src:]
    if last:
        before_ref, rest = rest[0], rest[1:]
    n_out = len(rest) - 5
    outs = rest[:n_out]
    doc_ref, weights_ref, list_ref, buf_ref, sems = rest[n_out:]
    tpi, edge = buf_ref.shape[1], buf_ref.shape[3]
    chip, core = place_ref[0] // 2, place_ref[0] % 2
    blocks = sources[0].shape[0]

    count = collect(lambda g: (abs(g // 2 - chip) == chips - 1) == last, group_ref, live_ref,
                    list_ref, tiles_ref, buf_ref, sems)
    if last:
        doc_ref[...] = before_ref[...]
    else:
        doc_ref[...] = jnp.zeros_like(doc_ref)
    for source, (hops, other, piece) in zip(sources, away):
        there = chip + hops

        @pl.when((there >= 0) & (there < chips))
        def _():
            owner = there * 2 + (core if other == 0 else 1 - core)
            weights_ref[pl.ds(owner * owned + piece * blocks, blocks)] = source[...]

    def work(strip, at, valid):
        left = weights_ref[group_ref[strip] * owned + slot_ref[strip]]
        right = jnp.concatenate([buf_ref[at, j] for j in range(tpi)], axis=1)
        out = jnp.dot(left, right, preferred_element_type=F32) * valid
        for j in range(tpi):
            doc_ref[col_ref[strip, j]] += out[:, j * edge:(j + 1) * edge]

    in_batches(count, list_ref, tiles_ref, buf_ref, sems, work)
    if not last:
        outs[0][...] = doc_ref[...]
    else:
        n_dev = len(outs)
        held = outs[0].shape[0]
        for s in range(n_dev):
            at = partner_of(n_dev, place_ref[1], s) * held
            outs[s][...] = doc_ref[pl.ds(at, held)].astype(outs[s].dtype)


def project(last, scalars, tiles, sources, away, before, chips, owned, n_dev, held):
    strips, tpi, edge, _ = tiles.shape
    cols = sources[0].shape[1]
    if last:
        out_shape = [pltpu.VMEM((held, cols, edge), BF16 if s else F32) for s in range(n_dev)]
    else:
        out_shape = [pltpu.VMEM((n_dev * held, cols, edge), F32)]
    more = [near(before)] if last else []
    return pl.pallas_call(
        functools.partial(project_kernel, last, chips, owned, away),
        out_shape=out_shape,
        in_specs=[SM] * 5 + [HB] + [VM] * (len(sources) + len(more)),
        out_specs=[VM] * len(out_shape),
        scratch_shapes=[
            pltpu.VMEM((n_dev * held, cols, edge), F32),
            pltpu.VMEM((2 * chips * owned, cols, edge), BF16),
            pltpu.SMEM((strips,), jnp.int32),
            pltpu.VMEM((strips, tpi, edge, edge), BF16),
            pltpu.SemaphoreType.DMA((strips,)),
        ],
        compiler_params=params(28),
        cost_estimate=cost(strips // 4 if last else strips),
        name="project_last" if last else "project",
    )(*scalars, far_off(tiles), *[near(s) for s in sources], *more)


def finish_kernel(inverse_ref, own_ref, *rest):
    arrived, out_ref = rest[:-1], rest[-1]
    blocks, _, edge = own_ref.shape
    for b in range(blocks):
        total = own_ref[b]
        for r in arrived:
            total += r[b].astype(F32)
        out_ref[:, b * edge:(b + 1) * edge] = jnp.dot(
            inverse_ref[...], total, precision=HIGHEST, preferred_element_type=F32).astype(BF16)


def on_chip(kernel, out_shape, *args, in_specs=None, scratch=(), mib=8):
    specs = in_specs or [VM] * len(args)
    return pl.pallas_call(
        kernel, out_shape=out_shape, in_specs=specs,
        out_specs=jax.tree.map(lambda _: VM, out_shape,
                               is_leaf=lambda x: not isinstance(x, (tuple, list))),
        scratch_shapes=list(scratch), compiler_params=params(mib),
    )(*[near(a) if s is VM else a for a, s in zip(args, specs)])


def partner_of(n, me, s, back=False):
    if n & (n - 1) == 0:
        return me ^ s
    return (me + (n - s if back else s)) % n


def partners(n, s):
    return [(i, partner_of(n, i, s)) for i in range(n)]


def sum_over(x, axis, n, least=1):
    s = least
    while s < n:
        width = min(4, n // s)
        others = []
        for k in range(1, width):
            others.append(lax.ppermute(
                x, axis, [(i, i // (s * width) * (s * width)
                           + (i + k * s) % (s * width)) for i in range(n)]))
        for other in others:
            x = x + other
        s *= width
    return x


def on_device(tiles, tile_col, strip_group, strip_slot, live_count, omega, idf):
    n_group = lax.axis_size("group")
    n_dev = lax.axis_size("dev")
    chips = n_group // 2
    edge = tiles.shape[2]
    cols = omega.shape[1]
    owned = idf.shape[0] // edge
    pieces = 2 if owned % 2 == 0 else 1
    blocks = owned // pieces
    me, band = lax.axis_index("group"), lax.axis_index("dev")
    place = jnp.stack([me, band]).astype(jnp.int32)
    scalars = (strip_group, strip_slot, tile_col, live_count, place)
    swap = lambda x: lax.ppermute(x, "group", [(i, i ^ 1) for i in range(n_group)])

    def along(x, links):
        return lax.ppermute(
            x, "group", [(2 * a + k, 2 * b + k) for a, b in links for k in (0, 1)])

    col_own = omega.shape[0] // edge
    own_omega = omega.reshape(col_own, edge, cols)
    omegas = [own_omega] + [lax.ppermute(own_omega, "dev", partners(n_dev, s))
                            for s in range(1, n_dev)]

    far_mine, far_theirs = partial_sketch(True, scalars, tiles, omegas, chips, owned)
    far_pair = swap(far_theirs)
    piece_shape = pltpu.VMEM((blocks, edge, cols), BF16)
    first = [on_chip(functools.partial(first_kernel, blocks, p), piece_shape,
                     far_mine, far_pair) for p in range(pieces)]
    ends = [(0, 1), (chips - 1, chips - 2)]
    ups = [along(x, ends) for x in first]
    downs = list(ups) if chips > 2 else [jnp.zeros_like(x) for x in ups]
    rest_mine, rest_theirs = partial_sketch(False, scalars, tiles, omegas, chips, owned, first)
    rest_pair = swap(rest_theirs)
    for t in range(2, chips):
        up_links = [(c, c + 1) for c in range(t)]
        down_links = [(chips - 1 - a, chips - 1 - b) for a, b in up_links]
        for p in range(pieces):
            to_up, to_down = on_chip(
                functools.partial(relay_kernel, t, chips, owned, blocks, p),
                (piece_shape, piece_shape), place, far_mine, far_pair, rest_mine,
                rest_pair, ups[p], downs[p], in_specs=[SM] + [VM] * 6)
            ups[p] = along(to_up, up_links)
            downs[p] = along(to_down, down_links)

    gram = jnp.zeros((cols, cols), F32)
    sketches, weights = [], []
    for p in range(pieces):
        sk, w, gram = on_chip(
            functools.partial(combine_kernel, chips, owned, p),
            (pltpu.VMEM((blocks, edge, cols), F32), pltpu.VMEM((blocks, cols, edge), BF16),
             pltpu.VMEM((cols, cols), F32)),
            place, rest_mine, rest_pair, ups[p], downs[p], idf.reshape(owned, edge),
            gram, in_specs=[SM] + [VM] * 6)
        sketches.append(sk)
        weights.append(w)

    up_links = [(c, c + 1) for c in range(chips - 1)]
    down_links = [(c + 1, c) for c in range(chips - 1)]
    sources, away = [], []
    for p in range(pieces):
        sources += [weights[p], swap(weights[p])]
        away += [(0, 0, p), (0, 1, p)]
    below, above = list(weights), list(weights)
    for t in range(1, chips):
        if t == chips - 1:
            near_sources, near_away, sources, away = sources, away, [], []
        for p in range(pieces):
            below[p] = along(below[p], up_links)
            above[p] = along(above[p], down_links)
        for p in range(pieces):
            sources += [below[p], swap(below[p]), above[p], swap(above[p])]
            away += [(-t, 0, p), (-t, 1, p), (t, 0, p), (t, 1, p)]

    gram = sum_over(gram, "dev", n_dev)
    gram = gram + swap(gram)
    gram = sum_over(gram, "group", n_group, 2)
    inverse = on_chip(functools.partial(factor_kernel, idf.shape[0] * n_group * n_dev),
                      pltpu.VMEM((cols, cols), F32), gram,
                      scratch=[pltpu.VMEM((cols, cols), F32)])
    q_basis = on_chip(basis_kernel, jax.ShapeDtypeStruct((owned, edge, cols), F32),
                      inverse, *sketches).reshape(owned * edge, cols)

    docs = project(False, scalars, tiles, near_sources, near_away, None, chips, owned, n_dev,
                   col_own)[0]
    parts = project(True, scalars, tiles, sources, away, docs, chips, owned, n_dev, col_own)
    arrived = [lax.ppermute(parts[s], "dev", partners(n_dev, s)) for s in range(1, n_dev)]
    doc_factor = on_chip(finish_kernel, jax.ShapeDtypeStruct((cols, col_own * edge), BF16),
                         inverse, parts[0], *arrived)
    return (q_basis, doc_factor)


def solution(mesh):
    placed = (
        P(("group", "dev"), None, None, None),
        P(("group", "dev"), None),
        P(("group", "dev")),
        P(("group", "dev")),
        P(("group", "dev")),
        P(("group", "dev"), None),
        P(("group", "dev")),
    )

    return jax.shard_map(
        on_device,
        mesh=mesh,
        in_specs=placed,
        out_specs=(P(("group", "dev"), None), P(None, ("group", "dev"))),
        check_vma=False,
    )
```

```python
import functools
import jax
import jax.numpy as jnp
from jax import lax
from jax.experimental import pallas as pl
from jax.experimental.pallas import tpu as pltpu
from jax.sharding import PartitionSpec as P

F32 = jnp.float32
BF16 = jnp.bfloat16
HIGHEST = lax.Precision.HIGHEST
BATCH = 4
WIDE = 4

VM = pl.BlockSpec(memory_space=pltpu.VMEM)
SM = pl.BlockSpec(memory_space=pltpu.SMEM)
HB = pl.BlockSpec(memory_space=pltpu.HBM)


def near(x):
    return pltpu.with_memory_space_constraint(x, pltpu.VMEM)


def far_off(x):
    return pltpu.with_memory_space_constraint(x, pltpu.HBM)


def cost(strips):
    return pl.CostEstimate(flops=strips << 28, bytes_accessed=strips << 19, transcendentals=0)


def params(mib):
    return pltpu.CompilerParams(vmem_limit_bytes=mib << 20)


ME, BAND, LIVE, LISTS = 0, 1, 2, 3


class Ints:
    def __init__(self, ref, strips, tpi):
        self.ref, self.strips, self.tpi = ref, strips, tpi

    def me(self):
        return self.ref[ME]

    def band(self):
        return self.ref[BAND]

    def live(self):
        return self.ref[LIVE]

    def group(self, strip):
        return self.ref[LISTS + strip]

    def slot(self, strip):
        return self.ref[LISTS + self.strips + strip]

    def column(self, strip, j):
        return self.ref[LISTS + (2 + j) * self.strips + strip]


def far_chip(chip, chips):
    return jnp.where(chip < chips // 2, chips - 1, 0)


def lists_kernel(strips, tpi, chips, ints_ref, lists_ref):
    ints = Ints(ints_ref, strips, tpi)
    far = far_chip(ints.me() // 2, chips)

    def scan(strip, count):
        hit = ints.group(strip) // 2 == far
        lists_ref[jnp.where(hit, count, strips - 1 - strip + count)] = strip
        return count + hit.astype(jnp.int32)

    count = lax.fori_loop(0, ints.live(), scan, jnp.int32(0))
    lists_ref[strips] = count
    lists_ref[strips + 1] = ints.live() - count


class Picked:
    def __init__(self, lists_ref, strips, far, rest):
        n_far, n_rest = lists_ref[strips], lists_ref[strips + 1]
        self.lists, self.strips = lists_ref, strips
        self.start = jnp.where(rest, strips - n_rest, 0)
        self.count = jnp.where(far, n_far, 0) + jnp.where(rest, n_rest, 0)

    def strip(self, at):
        where = self.start + at
        return self.lists[jnp.where(where >= self.strips, where - self.strips, where)]

    def fetch(self, tiles_ref, buf_ref, sems):
        def begin(at, carry):
            pltpu.make_async_copy(tiles_ref.at[self.strip(at)], buf_ref.at[at],
                                  sems.at[at]).start()
            return carry

        lax.fori_loop(0, self.count, begin, jnp.int32(0))

    def in_batches(self, tiles_ref, buf_ref, sems, work):
        def trip(b, carry):
            for i in range(BATCH):
                at = b * BATCH + i

                @pl.when(at < self.count)
                def _():
                    pltpu.make_async_copy(tiles_ref.at[0], buf_ref.at[at], sems.at[at]).wait()

            for i in range(BATCH):
                at = jnp.minimum(b * BATCH + i, self.count - 1)
                work(self.strip(at), at, (b * BATCH + i < self.count).astype(F32))
            return carry

        lax.fori_loop(0, (self.count + BATCH - 1) // BATCH, trip, jnp.int32(0))


def sketch_kernel(far_only, chips, owned, n_src, ints_ref, lists_ref, tiles_ref, *rest):
    sources = rest[:n_src]
    both_ref, theirs_ref, omega_ref, buf_ref, sems = rest[-5:]
    half = theirs_ref.shape[0]
    strips, tpi = buf_ref.shape[:2]
    ints = Ints(ints_ref, strips, tpi)
    chip, core, band = ints.me() // 2, ints.me() % 2, ints.band()
    far = far_chip(chip, chips)
    held = sources[0].shape[0]
    own = pltpu.make_async_copy(sources[0], omega_ref.at[pl.ds(band * held, held)],
                                sems.at[strips])
    own.start()
    picked = Picked(lists_ref, strips, far_only, not far_only)
    picked.fetch(tiles_ref, buf_ref, sems)
    both_ref[...] = jnp.zeros_like(both_ref)
    for s in range(1, n_src):
        omega_ref[pl.ds(partner_of(n_src, band, s, back=True) * held, held)] = sources[s][...]
    own.wait()

    def work(strip, at, valid):
        owner = ints.group(strip)
        unit = jnp.int32(0) if far_only else owner // 2 - (far == 0).astype(jnp.int32)
        side = jnp.where(owner % 2 == core, 0, half)
        block = side + unit * owned + ints.slot(strip)
        left = jnp.concatenate([buf_ref[at, j] for j in range(tpi)], axis=1)
        right = jnp.concatenate([omega_ref[ints.column(strip, j)] for j in range(tpi)], axis=0)
        both_ref[block] += jnp.dot(left, right, preferred_element_type=F32) * valid

    picked.in_batches(tiles_ref, buf_ref, sems, work)
    theirs_ref[...] = both_ref[pl.ds(half, half)].astype(BF16)


def partial_sketch(far_only, scalars, tiles, sources, chips, owned, after=()):
    strips, tpi, edge, _ = tiles.shape
    col_own, _, cols = sources[0].shape
    blocks = owned * (1 if far_only else chips - 1)
    return pl.pallas_call(
        functools.partial(sketch_kernel, far_only, chips, owned, len(sources)),
        out_shape=(pltpu.VMEM((2 * blocks, edge, cols), F32),
                   pltpu.VMEM((blocks, edge, cols), BF16)),
        in_specs=[SM] * 2 + [HB] * 2 + [VM] * (len(sources) - 1 + len(after)),
        out_specs=(VM, VM),
        scratch_shapes=[
            pltpu.VMEM((col_own * len(sources), edge, cols), BF16),
            pltpu.VMEM((strips, tpi, edge, edge), BF16),
            pltpu.SemaphoreType.DMA((strips + 1,)),
        ],
        compiler_params=params(16),
        cost_estimate=cost(strips // 4 if far_only else strips),
        name="sketch_far" if far_only else "sketch_rest",
    )(*scalars, far_off(tiles), far_off(sources[0]),
      *[near(s) for s in (*sources[1:], *after)])


def first_kernel(blocks, piece, mine_ref, pair_ref, out_ref):
    rows = pl.ds(piece * blocks, blocks)
    out_ref[...] = (mine_ref[rows] + pair_ref[rows].astype(F32)).astype(BF16)


def relay_kernel(t, chips, owned, blocks, piece, ints_ref, far_mine, far_pair, rest_mine,
                 rest_pair, even_in, odd_in, even_out, odd_out):
    chip = ints_ref[ME] // 2
    far = far_chip(chip, chips)
    for parity in (0, 1):
        one_way = (chips - t + chip, chip > 0, (odd_in, even_in)[parity],
                   (even_out, odd_out)[parity])
        other_way = (t - chips + chip, chip < chips - 1, (even_in, odd_in)[parity],
                     (odd_out, even_out)[parity])
        for unit, fed, carried, out in (one_way, other_way):
            unit = jnp.clip(unit, 0, chips - 1)

            @pl.when((chip % 2 == parity) & (unit == far))
            def _():
                rows = pl.ds(piece * blocks, blocks)
                more = jnp.where(fed, carried[...].astype(F32), 0.0)
                out[...] = (far_mine[rows] + far_pair[rows].astype(F32) + more).astype(BF16)

            @pl.when((chip % 2 == parity) & (unit != far))
            def _():
                unit_at = unit - (far == 0).astype(jnp.int32)
                rows = pl.ds(unit_at * owned + piece * blocks, blocks)
                more = jnp.where(fed, carried[...].astype(F32), 0.0)
                out[...] = (rest_mine[rows] + rest_pair[rows].astype(F32) + more).astype(BF16)


def combine_kernel(chips, owned, piece, ints_ref, rest_mine, rest_pair, even_ref,
                   odd_ref, idf_ref, gram_in, sketch_ref, weight_ref, gram_ref):
    blocks = sketch_ref.shape[0]
    chip = ints_ref[ME] // 2
    unit_at = chip - (far_chip(chip, chips) == 0).astype(jnp.int32)
    inner = (chip > 0) & (chip < chips - 1)
    gram = gram_in[...]
    for b in range(blocks):
        at = unit_at * owned + piece * blocks + b
        total = (rest_mine[at] + rest_pair[at].astype(F32) + even_ref[b].astype(F32)
                 + jnp.where(inner, odd_ref[b].astype(F32), 0.0))
        row = idf_ref[pl.ds(piece * blocks + b, 1), :]
        scale = jnp.transpose(jnp.broadcast_to(row, total.shape[::-1]))
        sk = total * scale
        sketch_ref[b] = sk
        weight_ref[b] = jnp.transpose(sk * scale).astype(BF16)
        gram += lax.dot_general(sk, sk, (((0,), (0,)), ((), ())), precision=HIGHEST,
                                preferred_element_type=F32)
    gram_ref[...] = gram


def factor_kernel(total_terms, begin, end, *refs):
    x_ref = refs[-1]
    n = x_ref.shape[0]
    if begin == 0:
        x_ref[...] = refs[0][...] * (1.0 / total_terms)
    else:
        x_ref[...] = refs[0][...]
    rows = lax.broadcasted_iota(jnp.int32, (n, n), 0)
    columns = lax.broadcasted_iota(jnp.int32, (n, n), 1)

    lane = lax.broadcasted_iota(jnp.int32, (8, n), 1)

    def pick(values, at):
        return jnp.take_along_axis(values, jnp.full(values.shape, at, jnp.int32), axis=1)

    def eliminate(trip, carry):
        j = trip * WIDE
        x = x_ref[...]
        row = [jnp.broadcast_to(x_ref[pl.ds(j + k, 1), :], (8, n)) for k in range(WIDE)]
        column = [pick(x, j + k) for k in range(WIDE)]
        scaled = []
        for k in range(WIDE):
            here = lane == j + k
            scaled.append(jnp.where(here, 1.0, row[k]) / pick(row[k], j + k))
            for m in range(k + 1, WIDE):
                entry = pick(row[m], j + k)
                row[m] = jnp.where(here, 0.0, row[m]) - entry * scaled[k]
                column[m] = column[m] - column[k] * pick(scaled[k], j + m)[:1]
        below = rows >= j + WIDE
        x = jnp.where((columns >= j) & (columns < j + WIDE) & below, 0.0, x)
        for k in range(WIDE):
            passed = (lane > j + k) & (lane < j + WIDE)
            step = jnp.where(passed, 0.0, scaled[k])[:1]
            x = x - jnp.where(below, column[k], 0.0) * step
        x_ref[...] = x
        for k in range(WIDE):
            x_ref[pl.ds(j + k, 1), :] = row[k][:1]
        return carry

    lax.fori_loop(begin // WIDE, end // WIDE, eliminate, jnp.int32(0))
    if end == n:
        x = x_ref[...]
        pivots = jnp.sum(jnp.where(rows == columns, x, 0.0), axis=1, keepdims=True)
        lower = jnp.where(rows > columns, x, jnp.where(rows == columns, 1.0, 0.0))
        x_ref[...] = lower * lax.rsqrt(pivots)


def basis_kernel(inverse_ref, *rest):
    pieces, q_ref = rest[:-1], rest[-1]
    at = 0
    for piece in pieces:
        for b in range(piece.shape[0]):
            q_ref[at] = lax.dot_general(piece[b], inverse_ref[...], (((1,), (1,)), ((), ())),
                                        precision=HIGHEST, preferred_element_type=F32)
            at += 1


def project_kernel(last, chips, owned, away, ints_ref, lists_ref, tiles_ref, *rest):
    sources, rest = rest[:len(away)], rest[len(away):]
    before, outs = (rest[:1], rest[1:-4]) if last else ((), rest[:-4])
    doc_ref, weights_ref, buf_ref, sems = rest[-4:]
    strips, tpi, edge = buf_ref.shape[:3]
    ints = Ints(ints_ref, strips, tpi)
    chip, core = ints.me() // 2, ints.me() % 2
    at_end = abs(far_chip(chip, chips) - chip) == chips - 1
    picked = Picked(lists_ref, strips, at_end if last else jnp.logical_not(at_end), not last)
    picked.fetch(tiles_ref, buf_ref, sems)
    doc_ref[...] = before[0][...] if last else jnp.zeros_like(doc_ref)
    for source, (hops, other, piece) in zip(sources, away):
        there = chip + jnp.where(chip % 2 == 0, hops, -hops)
        size = source.shape[0]

        @pl.when((there >= 0) & (there < chips))
        def _():
            owner = there * 2 + (core if other == 0 else 1 - core)
            weights_ref[pl.ds(owner * owned + piece * size, size)] = source[...]

    def work(strip, at, valid):
        left = weights_ref[ints.group(strip) * owned + ints.slot(strip)]
        right = jnp.concatenate([buf_ref[at, j] for j in range(tpi)], axis=1)
        out = jnp.dot(left, right, preferred_element_type=F32) * valid
        for j in range(tpi):
            doc_ref[ints.column(strip, j)] += out[:, j * edge:(j + 1) * edge]

    picked.in_batches(tiles_ref, buf_ref, sems, work)
    if not last:
        outs[0][...] = doc_ref[...]
    else:
        n_dev, held = len(outs), outs[0].shape[0]
        for s in range(n_dev):
            at = partner_of(n_dev, ints.band(), s) * held
            outs[s][...] = doc_ref[pl.ds(at, held)].astype(outs[s].dtype)


def project(last, scalars, tiles, sources, away, before, chips, owned, n_dev, held):
    strips, tpi, edge, _ = tiles.shape
    cols = sources[0].shape[1]
    if last:
        out_shape = [pltpu.VMEM((held, cols, edge), BF16 if s else F32) for s in range(n_dev)]
    else:
        out_shape = [pltpu.VMEM((n_dev * held, cols, edge), F32)]
    more = [near(before)] if last else []
    return pl.pallas_call(
        functools.partial(project_kernel, last, chips, owned, away),
        out_shape=out_shape,
        in_specs=[SM] * 2 + [HB] + [VM] * (len(sources) + len(more)),
        out_specs=[VM] * len(out_shape),
        scratch_shapes=[
            pltpu.VMEM((n_dev * held, cols, edge), F32),
            pltpu.VMEM((2 * chips * owned, cols, edge), BF16),
            pltpu.VMEM((strips, tpi, edge, edge), BF16),
            pltpu.SemaphoreType.DMA((strips,)),
        ],
        compiler_params=params(28),
        cost_estimate=cost(strips // 4 if last else strips),
        name="project_last" if last else "project",
    )(*scalars, far_off(tiles), *[near(s) for s in sources], *more)


def finish_kernel(inverse_ref, own_ref, *rest):
    arrived, out_ref = rest[:-1], rest[-1]
    blocks, _, edge = own_ref.shape
    for b in range(blocks):
        total = own_ref[b]
        for r in arrived:
            total += r[b].astype(F32)
        out_ref[:, b * edge:(b + 1) * edge] = jnp.dot(
            inverse_ref[...], total, precision=HIGHEST, preferred_element_type=F32).astype(BF16)


def on_chip(kernel, out_shape, *args, in_specs=None, scratch=(), mib=8):
    specs = in_specs or [VM] * len(args)
    return pl.pallas_call(
        kernel, out_shape=out_shape, in_specs=specs,
        out_specs=jax.tree.map(lambda _: VM, out_shape,
                               is_leaf=lambda x: not isinstance(x, (tuple, list))),
        scratch_shapes=list(scratch), compiler_params=params(mib),
    )(*[near(a) if s is VM else a for a, s in zip(args, specs)])


def partner_of(n, me, s, back=False):
    if n & (n - 1) == 0:
        return me ^ s
    return (me + (n - s if back else s)) % n


def partners(n, s):
    return [(i, partner_of(n, i, s)) for i in range(n)]


def exchanges(x, axis, n, least=1):
    s, terms = least, [x]
    while s < n:
        x = functools.reduce(jnp.add, terms)
        width = min(4, n // s)
        span = s * width
        terms = [x] + [lax.ppermute(x, axis, [(i, i // span * span + (i + k * s) % span)
                                              for i in range(n)]) for k in range(1, width)]
        s = span
    return terms


def on_device(tiles, tile_col, strip_group, strip_slot, live_count, omega, idf):
    n_group = lax.axis_size("group")
    n_dev = lax.axis_size("dev")
    chips = n_group // 2
    edge = tiles.shape[2]
    cols = omega.shape[1]
    owned = idf.shape[0] // edge
    pieces = 2 if owned % 2 == 0 else 1
    blocks = owned // pieces
    me, band = lax.axis_index("group"), lax.axis_index("dev")
    strips, tpi = tile_col.shape
    ints = jnp.concatenate([me[None], band[None], live_count, strip_group, strip_slot]
                           + [tile_col[:, j] for j in range(tpi)]).astype(jnp.int32)
    lists = pl.pallas_call(
        functools.partial(lists_kernel, strips, tpi, chips),
        out_shape=jax.ShapeDtypeStruct((strips + 2,), jnp.int32), in_specs=[SM], out_specs=SM,
        name="lists")(ints)
    ints, lists = far_off(ints), far_off(lists)
    scalars = (ints, lists)
    swap_links = [(i, i ^ 1) for i in range(n_group)]

    def swap(x):
        return lax.ppermute(x, "group", swap_links)

    even_links = [(2 * c + k, 2 * (c ^ 1) + k) for c in range(chips) for k in (0, 1)]
    odd_links = []
    for c in range(chips):
        to = c + 1 if c % 2 else c - 1
        for k in (0, 1):
            odd_links.append((2 * c + k, 2 * to + k if 0 <= to < chips else 2 * c + 1 - k))

    def over(x, links):
        return lax.ppermute(x, "group", links)

    col_own = omega.shape[0] // edge
    own_omega = omega.reshape(col_own, edge, cols)
    omegas = [own_omega] + [lax.ppermute(own_omega, "dev", partners(n_dev, s))
                            for s in range(1, n_dev)]

    far_mine, far_theirs = partial_sketch(True, scalars, tiles, omegas, chips, owned)
    far_pair = swap(far_theirs)
    piece_shape = pltpu.VMEM((blocks, edge, cols), BF16)
    first = [on_chip(functools.partial(first_kernel, blocks, p), piece_shape,
                     far_mine, far_pair) for p in range(pieces)]
    evens = [over(x, even_links) for x in first]
    odds = list(evens)
    rest_mine, rest_theirs = partial_sketch(False, scalars, tiles, omegas, chips, owned, first)
    rest_pair = swap(rest_theirs)
    for t in range(2, chips):
        for p in range(pieces):
            to_even, to_odd = on_chip(
                functools.partial(relay_kernel, t, chips, owned, blocks, p),
                (piece_shape, piece_shape), ints, far_mine, far_pair, rest_mine,
                rest_pair, evens[p], odds[p], in_specs=[SM] + [VM] * 6)
            evens[p] = over(to_even, even_links)
            odds[p] = over(to_odd, odd_links)

    gram = jnp.zeros((cols, cols), F32)
    sketches, weights = [], []
    for p in range(pieces):
        sk, w, gram = on_chip(
            functools.partial(combine_kernel, chips, owned, p),
            (pltpu.VMEM((blocks, edge, cols), F32), pltpu.VMEM((blocks, cols, edge), BF16),
             pltpu.VMEM((cols, cols), F32)),
            ints, rest_mine, rest_pair, evens[p], odds[p],
            idf.reshape(owned, edge), gram, in_specs=[SM] + [VM] * 6)
        sketches.append(sk)
        weights.append(w)

    evens, odds = list(weights), list(weights)
    sources, away = [], []
    for p in range(pieces):
        sources += [weights[p], swap(weights[p])]
        away += [(0, 0, p), (0, 1, p)]
    for t in range(1, chips):
        if t == chips - 1:
            near_sources, near_away, sources, away = sources, away, [], []
        for p in range(pieces):
            to_even, to_odd = odds[p], evens[p]
            evens[p] = over(to_even, even_links)
            sources += [evens[p], swap(evens[p])]
            away += [(t, 0, p), (t, 1, p)]
            if t < chips - 1:
                odds[p] = over(to_odd, odd_links)
                sources += [odds[p], swap(odds[p])]
                away += [(-t, 0, p), (-t, 1, p)]

    near_chip = 2
    while near_chip < n_group:
        gram = gram + lax.ppermute(gram, "group", partners(n_group, near_chip))
        near_chip *= 2
    gram = functools.reduce(jnp.add, exchanges(gram, "dev", n_dev))
    gram = gram + swap(gram)
    square = pltpu.VMEM((cols, cols), F32)
    total = idf.shape[0] * n_group * n_dev
    inverse = on_chip(functools.partial(factor_kernel, total, 0, cols // 2), square,
                      gram)
    inverse = on_chip(functools.partial(factor_kernel, total, cols // 2, cols), square,
                      inverse)
    q_basis = on_chip(basis_kernel, jax.ShapeDtypeStruct((owned, edge, cols), F32),
                      inverse, *sketches).reshape(owned * edge, cols)

    docs = project(False, scalars, tiles, near_sources, near_away, None, chips, owned, n_dev,
                   col_own)[0]
    parts = project(True, scalars, tiles, sources, away, docs, chips, owned, n_dev, col_own)
    arrived = [lax.ppermute(parts[s], "dev", partners(n_dev, s)) for s in range(1, n_dev)]
    doc_factor = on_chip(finish_kernel, jax.ShapeDtypeStruct((cols, col_own * edge), BF16),
                         inverse, parts[0], *arrived)
    return (q_basis, doc_factor)


def solution(mesh):
    placed = (
        P(("group", "dev"), None, None, None),
        P(("group", "dev"), None),
        P(("group", "dev")),
        P(("group", "dev")),
        P(("group", "dev")),
        P(("group", "dev"), None),
        P(("group", "dev")),
    )

    return jax.shard_map(
        on_device,
        mesh=mesh,
        in_specs=placed,
        out_specs=(P(("group", "dev"), None), P(None, ("group", "dev"))),
        check_vma=False,
    )
```

```python
import functools
import jax
import jax.numpy as jnp
from jax import lax
from jax.experimental import pallas as pl
from jax.experimental.pallas import tpu as pltpu
from jax.sharding import PartitionSpec as P

F32 = jnp.float32
BF16 = jnp.bfloat16
HIGH = lax.Precision.HIGH
HIGHEST = lax.Precision.HIGHEST
BATCH = 4
WIDE = 4
PIECES = 2

VM = pl.BlockSpec(memory_space=pltpu.VMEM)
SM = pl.BlockSpec(memory_space=pltpu.SMEM)
HB = pl.BlockSpec(memory_space=pltpu.HBM)


def near(x):
    return pltpu.with_memory_space_constraint(x, pltpu.VMEM)


def far_off(x):
    return pltpu.with_memory_space_constraint(x, pltpu.HBM)


def cost(strips):
    return pl.CostEstimate(flops=strips << 28, bytes_accessed=strips << 19, transcendentals=0)


def params(mib):
    return pltpu.CompilerParams(vmem_limit_bytes=mib << 20)


ME, BAND, LIVE, LISTS = 0, 1, 2, 3


class Ints:
    def __init__(self, ref, strips, tpi):
        self.ref, self.strips, self.tpi = ref, strips, tpi

    def me(self):
        return self.ref[ME]

    def band(self):
        return self.ref[BAND]

    def live(self):
        return self.ref[LIVE]

    def group(self, strip):
        return self.ref[LISTS + strip]

    def slot(self, strip):
        return self.ref[LISTS + self.strips + strip]

    def column(self, strip, j):
        return self.ref[LISTS + (2 + j) * self.strips + strip]


def far_chip(chip, chips):
    return jnp.where(chip < chips // 2, chips - 1, 0)


CLASSES = 5


def lists_kernel(strips, tpi, chips, ints_ref, lists_ref):
    ints = Ints(ints_ref, strips, tpi)
    chip = ints.me() // 2
    far = far_chip(chip, chips)

    def scan(strip, counts):
        owner = ints.group(strip) // 2
        hops = abs(owner - chip)
        is_far, is_last, is_near = owner == far, hops == chips - 1, hops <= 1
        n_far, n_near, n_last = counts
        n_mid = strip - n_near - n_last
        lists_ref[jnp.where(is_far, n_far, strips + strip - n_far)] = strip
        lists_ref[jnp.where(is_near, 2 * strips + n_near,
                            jnp.where(is_last, 4 * strips + n_last, 3 * strips + n_mid))] = strip
        return tuple(n + hit.astype(jnp.int32)
                     for n, hit in zip(counts, (is_far, is_near, is_last)))

    n_far, n_near, n_last = lax.fori_loop(0, ints.live(), scan, (jnp.int32(0),) * 3)
    n_all = ints.live()
    for c, count in enumerate((n_far, n_all - n_far, n_near, n_all - n_near - n_last, n_last)):
        lists_ref[CLASSES * strips + c] = count


class Picked:
    def __init__(self, lists_ref, strips, own):
        self.lists, self.start = lists_ref, own * strips
        self.count = lists_ref[CLASSES * strips + own]

    def strip(self, at):
        return self.lists[self.start + at]

    def fetch(self, tiles_ref, buf_ref, sems):
        def begin(at, carry):
            pltpu.make_async_copy(tiles_ref.at[self.strip(at)], buf_ref.at[at],
                                  sems.at[at]).start()
            return carry

        lax.fori_loop(0, self.count, begin, jnp.int32(0))

    def in_batches(self, tiles_ref, buf_ref, sems, work):
        def trip(b, carry):
            for i in range(BATCH):
                at = b * BATCH + i

                @pl.when(at < self.count)
                def _():
                    pltpu.make_async_copy(tiles_ref.at[0], buf_ref.at[at], sems.at[at]).wait()

            for i in range(BATCH):
                at = jnp.minimum(b * BATCH + i, self.count - 1)
                work(self.strip(at), at, (b * BATCH + i < self.count).astype(F32))
            return carry

        lax.fori_loop(0, (self.count + BATCH - 1) // BATCH, trip, jnp.int32(0))


def sketch_kernel(far_only, chips, blocks, n_src, ints_ref, lists_ref, tiles_ref, *rest):
    sources = rest[:n_src]
    both_ref, *theirs, omega_ref, buf_ref, sems = rest[-3 - 1 - (1 if far_only else PIECES):]
    half = both_ref.shape[0] // 2
    units = half // (PIECES * blocks)
    strips, tpi = buf_ref.shape[:2]
    ints = Ints(ints_ref, strips, tpi)
    chip, core, band = ints.me() // 2, ints.me() % 2, ints.band()
    far = far_chip(chip, chips)
    held = sources[0].shape[0]
    own = pltpu.make_async_copy(sources[0], omega_ref.at[pl.ds(band * held, held)],
                                sems.at[strips])
    own.start()
    picked = Picked(lists_ref, strips, 0 if far_only else 1)
    picked.fetch(tiles_ref, buf_ref, sems)
    both_ref[...] = jnp.zeros_like(both_ref)
    for s in range(1, n_src):
        omega_ref[pl.ds(partner_of(n_src, band, s, back=True) * held, held)] = sources[s][...]
    own.wait()

    def work(strip, at, valid):
        owner = ints.group(strip)
        unit = jnp.int32(0) if far_only else owner // 2 - (far == 0).astype(jnp.int32)
        side = jnp.where(owner % 2 == core, 0, half)
        piece, slot = ints.slot(strip) // blocks, ints.slot(strip) % blocks
        block = side + (piece * units + unit) * blocks + slot
        left = jnp.concatenate([buf_ref[at, j] for j in range(tpi)], axis=1)
        right = jnp.concatenate([omega_ref[ints.column(strip, j)] for j in range(tpi)], axis=0)
        both_ref[block] += jnp.dot(left, right, preferred_element_type=F32) * valid

    picked.in_batches(tiles_ref, buf_ref, sems, work)
    size = half // len(theirs)
    for p, out in enumerate(theirs):
        out[...] = both_ref[pl.ds(half + p * size, size)].astype(BF16)


def partial_sketch(far_only, scalars, tiles, sources, chips, blocks, after=()):
    strips, tpi, edge, _ = tiles.shape
    col_own, _, cols = sources[0].shape
    half = PIECES * blocks * (1 if far_only else chips - 1)
    n_out = 1 if far_only else PIECES
    return pl.pallas_call(
        functools.partial(sketch_kernel, far_only, chips, blocks, len(sources)),
        out_shape=(pltpu.VMEM((2 * half, edge, cols), F32),)
        + (pltpu.VMEM((half // n_out, edge, cols), BF16),) * n_out,
        in_specs=[SM] * 2 + [HB] * 2 + [VM] * (len(sources) - 1 + len(after)),
        out_specs=(VM,) * (1 + n_out),
        scratch_shapes=[
            pltpu.VMEM((col_own * len(sources), edge, cols), BF16),
            pltpu.VMEM((strips, tpi, edge, edge), BF16),
            pltpu.SemaphoreType.DMA((strips + 1,)),
        ],
        compiler_params=params(16),
        cost_estimate=cost(strips // 4 if far_only else strips),
        name="sketch_far" if far_only else "sketch_rest",
    )(*scalars, far_off(tiles), far_off(sources[0]),
      *[near(s) for s in (*sources[1:], *after)])


def first_kernel(blocks, piece, mine_ref, pair_ref, out_ref):
    rows = pl.ds(piece * blocks, blocks)
    out_ref[...] = (mine_ref[rows] + pair_ref[rows].astype(F32)).astype(BF16)


def relay_kernel(t, chips, blocks, piece, ints_ref, far_mine, far_pair, rest_mine,
                 rest_pair, even_in, odd_in, even_out, odd_out):
    chip = ints_ref[ME] // 2
    far = far_chip(chip, chips)
    for parity in (0, 1):
        one_way = (chips - t + chip, chip > 0, (odd_in, even_in)[parity],
                   (even_out, odd_out)[parity])
        other_way = (t - chips + chip, chip < chips - 1, (even_in, odd_in)[parity],
                     (odd_out, even_out)[parity])
        for unit, fed, carried, out in (one_way, other_way):
            unit = jnp.clip(unit, 0, chips - 1)

            @pl.when((chip % 2 == parity) & (unit == far))
            def _():
                rows = pl.ds(piece * blocks, blocks)
                more = jnp.where(fed, carried[...].astype(F32), 0.0)
                out[...] = (far_mine[rows] + far_pair[rows].astype(F32) + more).astype(BF16)

            @pl.when((chip % 2 == parity) & (unit != far))
            def _():
                unit_at = unit - (far == 0).astype(jnp.int32)
                rows = pl.ds((piece * (chips - 1) + unit_at) * blocks, blocks)
                there = pl.ds(unit_at * blocks, blocks)
                more = jnp.where(fed, carried[...].astype(F32), 0.0)
                out[...] = (rest_mine[rows] + rest_pair[there].astype(F32) + more).astype(BF16)


def combine_kernel(chips, piece, ints_ref, rest_mine, rest_pair, even_ref,
                   odd_ref, idf_ref, gram_in, sketch_ref, weight_ref, gram_ref):
    blocks = sketch_ref.shape[0]
    chip = ints_ref[ME] // 2
    unit_at = chip - (far_chip(chip, chips) == 0).astype(jnp.int32)
    inner = (chip > 0) & (chip < chips - 1)
    gram = gram_in[...]
    for b in range(blocks):
        at = unit_at * blocks + b
        total = (rest_mine[piece * (chips - 1) * blocks + at] + rest_pair[at].astype(F32) + even_ref[b].astype(F32)
                 + jnp.where(inner, odd_ref[b].astype(F32), 0.0))
        row = idf_ref[pl.ds(piece * blocks + b, 1), :]
        scale = jnp.transpose(jnp.broadcast_to(row, total.shape[::-1]))
        sk = total * scale
        sketch_ref[b] = sk
        weight_ref[b] = jnp.transpose(sk * scale).astype(BF16)
        gram += lax.dot_general(sk, sk, (((0,), (0,)), ((), ())), precision=HIGHEST,
                                preferred_element_type=F32)
    gram_ref[...] = gram


def factor_kernel(total_terms, begin, end, *refs):
    x_ref = refs[-1]
    n = x_ref.shape[0]
    if begin == 0:
        x_ref[...] = refs[0][...] * (1.0 / total_terms)
    else:
        x_ref[...] = refs[0][...]
    rows = lax.broadcasted_iota(jnp.int32, (n, n), 0)
    columns = lax.broadcasted_iota(jnp.int32, (n, n), 1)

    lane = lax.broadcasted_iota(jnp.int32, (8, n), 1)

    def pick(values, at):
        return jnp.take_along_axis(values, jnp.full(values.shape, at, jnp.int32), axis=1)

    def eliminate(trip, carry):
        j = trip * WIDE
        x = x_ref[...]
        row = [jnp.broadcast_to(x_ref[pl.ds(j + k, 1), :], (8, n)) for k in range(WIDE)]
        column = [pick(x, j + k) for k in range(WIDE)]
        block = [[pick(row[k], j + m) for m in range(WIDE)] for k in range(WIDE)]
        scaled = []
        for k in range(WIDE):
            here = lane == j + k
            inverse = 1.0 / block[k][k]
            scaled.append(jnp.where(here, 1.0, row[k]) * inverse)
            for m in range(k + 1, WIDE):
                entry, across = block[m][k], block[k][m] * inverse
                for i in range(k + 1, WIDE):
                    block[m][i] = block[m][i] - entry * (block[k][i] * inverse)
                row[m] = jnp.where(here, 0.0, row[m]) - entry * scaled[k]
                column[m] = column[m] - column[k] * across[:1]
        below = rows >= j + WIDE
        x = jnp.where((columns >= j) & (columns < j + WIDE) & below, 0.0, x)
        for k in range(WIDE):
            passed = (lane > j + k) & (lane < j + WIDE)
            step = jnp.where(passed, 0.0, scaled[k])[:1]
            x = x - jnp.where(below, column[k], 0.0) * step
        x_ref[...] = x
        for k in range(WIDE):
            x_ref[pl.ds(j + k, 1), :] = row[k][:1]
        return carry

    lax.fori_loop(begin // WIDE, end // WIDE, eliminate, jnp.int32(0))
    if end == n:
        x = x_ref[...]
        pivots = jnp.sum(jnp.where(rows == columns, x, 0.0), axis=1, keepdims=True)
        lower = jnp.where(rows > columns, x, jnp.where(rows == columns, 1.0, 0.0))
        x_ref[...] = lower * lax.rsqrt(pivots)


def basis_kernel(inverse_ref, *rest):
    pieces, q_ref = rest[:-1], rest[-1]
    at = 0
    for piece in pieces:
        for b in range(piece.shape[0]):
            q_ref[at] = lax.dot_general(piece[b], inverse_ref[...], (((1,), (1,)), ((), ())),
                                        precision=HIGH, preferred_element_type=F32)
            at += 1


def project_kernel(own_class, chips, owned, away, ints_ref, lists_ref, tiles_ref, *rest):
    sources, rest = rest[:len(away)], rest[len(away):]
    last = own_class == 2
    n_more = 1 if own_class else 0
    before, outs = rest[:n_more], rest[n_more:-4]
    doc_ref, weights_ref, buf_ref, sems = rest[-4:]
    strips, tpi, edge = buf_ref.shape[:3]
    ints = Ints(ints_ref, strips, tpi)
    chip, core = ints.me() // 2, ints.me() % 2
    picked = Picked(lists_ref, strips, 2 + own_class)
    picked.fetch(tiles_ref, buf_ref, sems)
    doc_ref[...] = before[0][...] if n_more else jnp.zeros_like(doc_ref)
    for source, (hops, other, piece) in zip(sources, away):
        there = chip + jnp.where(chip % 2 == 0, hops, -hops)
        size = source.shape[0]

        @pl.when((there >= 0) & (there < chips))
        def _():
            owner = there * 2 + (core if other == 0 else 1 - core)
            weights_ref[pl.ds(owner * owned + piece * size, size)] = source[...]

    def work(strip, at, valid):
        left = weights_ref[ints.group(strip) * owned + ints.slot(strip)]
        right = jnp.concatenate([buf_ref[at, j] for j in range(tpi)], axis=1)
        out = jnp.dot(left, right, preferred_element_type=F32) * valid
        for j in range(tpi):
            doc_ref[ints.column(strip, j)] += out[:, j * edge:(j + 1) * edge]

    picked.in_batches(tiles_ref, buf_ref, sems, work)
    if not last:
        outs[0][...] = doc_ref[...]
    else:
        n_dev, held = len(outs), outs[0].shape[0]
        for s in range(n_dev):
            at = partner_of(n_dev, ints.band(), s) * held
            outs[s][...] = doc_ref[pl.ds(at, held)].astype(outs[s].dtype)


def project(own_class, scalars, tiles, sources, away, before, chips, owned, n_dev, held):
    strips, tpi, edge, _ = tiles.shape
    cols = sources[0].shape[1]
    last = own_class == 2
    if last:
        out_shape = [pltpu.VMEM((held, cols, edge), BF16 if s else F32) for s in range(n_dev)]
    else:
        out_shape = [pltpu.VMEM((n_dev * held, cols, edge), F32)]
    more = [near(before)] if own_class else []
    return pl.pallas_call(
        functools.partial(project_kernel, own_class, chips, owned, away),
        out_shape=out_shape,
        in_specs=[SM] * 2 + [HB] + [VM] * (len(sources) + len(more)),
        out_specs=[VM] * len(out_shape),
        scratch_shapes=[
            pltpu.VMEM((n_dev * held, cols, edge), F32),
            pltpu.VMEM((2 * chips * owned, cols, edge), BF16),
            pltpu.VMEM((strips, tpi, edge, edge), BF16),
            pltpu.SemaphoreType.DMA((strips,)),
        ],
        compiler_params=params(28),
        cost_estimate=cost(strips // 3),
    )(*scalars, far_off(tiles), *[near(s) for s in sources], *more)


def finish_kernel(inverse_ref, own_ref, *rest):
    arrived, out_ref = rest[:-1], rest[-1]
    blocks, _, edge = own_ref.shape
    for b in range(blocks):
        total = own_ref[b]
        for r in arrived:
            total += r[b].astype(F32)
        out_ref[:, b * edge:(b + 1) * edge] = jnp.dot(
            inverse_ref[...], total, precision=HIGHEST, preferred_element_type=F32).astype(BF16)


def on_chip(kernel, out_shape, *args, in_specs=None, scratch=(), mib=8):
    specs = in_specs or [VM] * len(args)
    return pl.pallas_call(
        kernel, out_shape=out_shape, in_specs=specs,
        out_specs=jax.tree.map(lambda _: VM, out_shape,
                               is_leaf=lambda x: not isinstance(x, (tuple, list))),
        scratch_shapes=list(scratch), compiler_params=params(mib),
    )(*[near(a) if s is VM else a for a, s in zip(args, specs)])


def partner_of(n, me, s, back=False):
    if n & (n - 1) == 0:
        return me ^ s
    return (me + (n - s if back else s)) % n


def partners(n, s):
    return [(i, partner_of(n, i, s)) for i in range(n)]


def exchanges(x, axis, n, least=1):
    s, terms = least, [x]
    while s < n:
        x = functools.reduce(jnp.add, terms)
        width = min(4, n // s)
        span = s * width
        terms = [x] + [lax.ppermute(x, axis, [(i, i // span * span + (i + k * s) % span)
                                              for i in range(n)]) for k in range(1, width)]
        s = span
    return terms


def on_device(tiles, tile_col, strip_group, strip_slot, live_count, omega, idf):
    n_group = lax.axis_size("group")
    n_dev = lax.axis_size("dev")
    chips = n_group // 2
    edge = tiles.shape[2]
    cols = omega.shape[1]
    owned = idf.shape[0] // edge
    pieces = PIECES
    blocks = owned // pieces
    me, band = lax.axis_index("group"), lax.axis_index("dev")
    strips, tpi = tile_col.shape
    ints = jnp.concatenate([me[None], band[None], live_count, strip_group, strip_slot]
                           + [tile_col[:, j] for j in range(tpi)]).astype(jnp.int32)
    ints = far_off(ints)

    lists = far_off(pl.pallas_call(
        functools.partial(lists_kernel, strips, tpi, chips),
        out_shape=jax.ShapeDtypeStruct((CLASSES * (strips + 1),), jnp.int32), in_specs=[SM],
        out_specs=SM, compiler_params=params(1), name="lists")(ints))
    scalars = (ints, lists)
    swap_links = [(i, i ^ 1) for i in range(n_group)]

    def swap(x):
        return lax.ppermute(x, "group", swap_links)

    even_links = [(2 * c + k, 2 * (c ^ 1) + k) for c in range(chips) for k in (0, 1)]
    odd_links = []
    for c in range(chips):
        to = c + 1 if c % 2 else c - 1
        for k in (0, 1):
            odd_links.append((2 * c + k, 2 * to + k if 0 <= to < chips else 2 * c + 1 - k))

    def over(x, links):
        return lax.ppermute(x, "group", links)

    col_own = omega.shape[0] // edge
    own_omega = omega.reshape(col_own, edge, cols)
    omegas = [own_omega] + [lax.ppermute(own_omega, "dev", partners(n_dev, s))
                            for s in range(1, n_dev)]

    far_mine, far_theirs = partial_sketch(True, scalars, tiles, omegas, chips, blocks)
    far_pair = swap(far_theirs)
    piece_shape = pltpu.VMEM((blocks, edge, cols), BF16)
    first = [on_chip(functools.partial(first_kernel, blocks, p), piece_shape,
                     far_mine, far_pair) for p in range(pieces)]
    evens = [over(x, even_links) for x in first]
    odds = list(evens)
    rest_mine, *rest_theirs = partial_sketch(False, scalars, tiles, omegas, chips, blocks,
                                             first)
    rest_pairs = [swap(x) for x in rest_theirs]
    for t in range(2, chips):
        for p in range(pieces):
            to_even, to_odd = on_chip(
                functools.partial(relay_kernel, t, chips, blocks, p),
                (piece_shape, piece_shape), ints, far_mine, far_pair, rest_mine,
                rest_pairs[p], evens[p], odds[p], in_specs=[SM] + [VM] * 6)
            evens[p] = over(to_even, even_links)
            odds[p] = over(to_odd, odd_links)

    gram = jnp.zeros((cols, cols), F32)
    sketches, weights = [], []
    for p in range(pieces):
        sk, w, gram = on_chip(
            functools.partial(combine_kernel, chips, p),
            (pltpu.VMEM((blocks, edge, cols), F32), pltpu.VMEM((blocks, cols, edge), BF16),
             pltpu.VMEM((cols, cols), F32)),
            ints, rest_mine, rest_pairs[p], evens[p], odds[p],
            idf.reshape(owned, edge), gram, in_specs=[SM] + [VM] * 6)
        sketches.append(sk)
        weights.append(w)

    evens, odds = list(weights), list(weights)
    sources, away = [], []
    for p in range(pieces):
        sources += [weights[p], swap(weights[p])]
        away += [(0, 0, p), (0, 1, p)]
    stages = []
    for t in range(1, chips):
        if t in (2, chips - 1):
            stages.append((sources, away))
            sources, away = [], []
        for p in range(pieces):
            to_even, to_odd = odds[p], evens[p]
            evens[p] = over(to_even, even_links)
            sources += [evens[p], swap(evens[p])]
            away += [(t, 0, p), (t, 1, p)]
            if t < chips - 1:
                odds[p] = over(to_odd, odd_links)
                sources += [odds[p], swap(odds[p])]
                away += [(-t, 0, p), (-t, 1, p)]
    stages.append((sources, away))

    step = 2
    while step < n_group:
        gram = gram + lax.ppermute(gram, "group", partners(n_group, step))
        step *= 2
    gram = functools.reduce(jnp.add, exchanges(gram, "dev", n_dev))
    gram = gram + swap(gram)
    square = pltpu.VMEM((cols, cols), F32)
    total = idf.shape[0] * n_group * n_dev
    inverse = on_chip(functools.partial(factor_kernel, total, 0, cols // 2), square,
                      gram)
    inverse = on_chip(functools.partial(factor_kernel, total, cols // 2, cols), square,
                      inverse)
    q_basis = on_chip(basis_kernel, jax.ShapeDtypeStruct((owned, edge, cols), F32),
                      inverse, *sketches).reshape(owned * edge, cols)

    docs = None
    for own_class, (sources, away) in enumerate(stages):
        docs = project(own_class, scalars, tiles, sources, away, docs, chips, owned, n_dev,
                       col_own)
        docs = docs if own_class == 2 else docs[0]
    parts = docs
    arrived = [lax.ppermute(parts[s], "dev", partners(n_dev, s)) for s in range(1, n_dev)]
    doc_factor = on_chip(finish_kernel, jax.ShapeDtypeStruct((cols, col_own * edge), BF16),
                         inverse, parts[0], *arrived)
    return (q_basis, doc_factor)


def solution(mesh):
    placed = (
        P(("group", "dev"), None, None, None),
        P(("group", "dev"), None),
        P(("group", "dev")),
        P(("group", "dev")),
        P(("group", "dev")),
        P(("group", "dev"), None),
        P(("group", "dev")),
    )

    return jax.shard_map(
        on_device,
        mesh=mesh,
        in_specs=placed,
        out_specs=(P(("group", "dev"), None), P(None, ("group", "dev"))),
        check_vma=False,
    )
```

```python
import functools
import jax
import jax.numpy as jnp
from jax import lax
from jax.experimental import pallas as pl
from jax.experimental.pallas import tpu as pltpu
from jax.sharding import PartitionSpec as P

F32 = jnp.float32
BF16 = jnp.bfloat16
HIGH = lax.Precision.HIGH
HIGHEST = lax.Precision.HIGHEST
BATCH = 4
WIDE = 4
PIECES = 2

VM = pl.BlockSpec(memory_space=pltpu.VMEM)
SM = pl.BlockSpec(memory_space=pltpu.SMEM)
HB = pl.BlockSpec(memory_space=pltpu.HBM)


def near(x):
    return pltpu.with_memory_space_constraint(x, pltpu.VMEM)


def far_off(x):
    return pltpu.with_memory_space_constraint(x, pltpu.HBM)


def cost(strips):
    return pl.CostEstimate(flops=strips << 28, bytes_accessed=strips << 19, transcendentals=0)


def params(mib):
    return pltpu.CompilerParams(vmem_limit_bytes=mib << 20)


ME, BAND, LIVE, LISTS = 0, 1, 2, 3


class Ints:
    def __init__(self, ref, strips, tpi):
        self.ref, self.strips, self.tpi = ref, strips, tpi

    def me(self):
        return self.ref[ME]

    def band(self):
        return self.ref[BAND]

    def live(self):
        return self.ref[LIVE]

    def group(self, strip):
        return self.ref[LISTS + strip]

    def slot(self, strip):
        return self.ref[LISTS + self.strips + strip]

    def column(self, strip, j):
        return self.ref[LISTS + (2 + j) * self.strips + strip]


def far_chip(chip, chips):
    return jnp.where(chip < chips // 2, chips - 1, 0)


CLASSES = 5


def lists_kernel(strips, tpi, chips, given_ref, ints_ref, lists_ref, sem):
    copy = pltpu.make_async_copy(given_ref, ints_ref, sem)
    copy.start()
    copy.wait()
    ints = Ints(ints_ref, strips, tpi)
    chip = ints.me() // 2
    far = far_chip(chip, chips)

    def scan(strip, counts):
        owner = ints.group(strip) // 2
        hops = abs(owner - chip)
        is_far, is_last, is_near = owner == far, hops == chips - 1, hops <= 1
        n_far, n_near, n_last = counts
        n_mid = strip - n_near - n_last
        lists_ref[jnp.where(is_far, n_far, strips + strip - n_far)] = strip
        lists_ref[jnp.where(is_near, 2 * strips + n_near,
                            jnp.where(is_last, 4 * strips + n_last, 3 * strips + n_mid))] = strip
        return tuple(n + hit.astype(jnp.int32)
                     for n, hit in zip(counts, (is_far, is_near, is_last)))

    n_far, n_near, n_last = lax.fori_loop(0, ints.live(), scan, (jnp.int32(0),) * 3)
    n_all = ints.live()
    for c, count in enumerate((n_far, n_all - n_far, n_near, n_all - n_near - n_last, n_last)):
        lists_ref[CLASSES * strips + c] = count


class Picked:
    def __init__(self, lists_ref, strips, own):
        self.lists, self.start = lists_ref, own * strips
        self.count = lists_ref[CLASSES * strips + own]

    def strip(self, at):
        return self.lists[self.start + at]

    def fetch(self, tiles_ref, buf_ref, sems):
        def begin(at, carry):
            pltpu.make_async_copy(tiles_ref.at[self.strip(at)], buf_ref.at[at],
                                  sems.at[at]).start()
            return carry

        lax.fori_loop(0, self.count, begin, jnp.int32(0))

    def in_batches(self, tiles_ref, buf_ref, sems, work, batch=BATCH):
        def trip(b, carry):
            for i in range(batch):
                at = b * batch + i

                @pl.when(at < self.count)
                def _():
                    pltpu.make_async_copy(tiles_ref.at[0], buf_ref.at[at], sems.at[at]).wait()

            for i in range(batch):
                at = jnp.minimum(b * batch + i, self.count - 1)
                work(self.strip(at), at, (b * batch + i < self.count).astype(F32))
            return carry

        lax.fori_loop(0, (self.count + batch - 1) // batch, trip, jnp.int32(0))


def sketch_kernel(far_only, chips, blocks, n_src, ints_ref, lists_ref, tiles_ref, *rest):
    sources = rest[:n_src]
    both_ref, *theirs, omega_ref, buf_ref, sems = rest[-3 - 1 - (1 if far_only else PIECES):]
    half = both_ref.shape[0] // 2
    units = half // (PIECES * blocks)
    strips, tpi = buf_ref.shape[:2]
    ints = Ints(ints_ref, strips, tpi)
    chip, core, band = ints.me() // 2, ints.me() % 2, ints.band()
    far = far_chip(chip, chips)
    held = sources[0].shape[0]
    own = pltpu.make_async_copy(sources[0], omega_ref.at[pl.ds(band * held, held)],
                                sems.at[strips])
    own.start()
    picked = Picked(lists_ref, strips, 0 if far_only else 1)
    picked.fetch(tiles_ref, buf_ref, sems)
    both_ref[...] = jnp.zeros_like(both_ref)
    for s in range(1, n_src):
        omega_ref[pl.ds(partner_of(n_src, band, s, back=True) * held, held)] = sources[s][...]
    own.wait()

    def work(strip, at, valid):
        owner = ints.group(strip)
        unit = jnp.int32(0) if far_only else owner // 2 - (far == 0).astype(jnp.int32)
        side = jnp.where(owner % 2 == core, 0, half)
        piece, slot = ints.slot(strip) // blocks, ints.slot(strip) % blocks
        block = side + (piece * units + unit) * blocks + slot
        left = jnp.concatenate([buf_ref[at, j] for j in range(tpi)], axis=1)
        right = jnp.concatenate([omega_ref[ints.column(strip, j)] for j in range(tpi)], axis=0)
        both_ref[block] += jnp.dot(left, right, preferred_element_type=F32) * valid

    picked.in_batches(tiles_ref, buf_ref, sems, work, BATCH if far_only else 2 * BATCH)
    size = half // len(theirs)
    for p, out in enumerate(theirs):
        out[...] = both_ref[pl.ds(half + p * size, size)].astype(BF16)


def partial_sketch(far_only, scalars, tiles, sources, chips, blocks, after=()):
    strips, tpi, edge, _ = tiles.shape
    col_own, _, cols = sources[0].shape
    half = PIECES * blocks * (1 if far_only else chips - 1)
    n_out = 1 if far_only else PIECES
    return pl.pallas_call(
        functools.partial(sketch_kernel, far_only, chips, blocks, len(sources)),
        out_shape=(pltpu.VMEM((2 * half, edge, cols), F32),)
        + (pltpu.VMEM((half // n_out, edge, cols), BF16),) * n_out,
        in_specs=[SM] * 2 + [HB] * 2 + [VM] * (len(sources) - 1 + len(after)),
        out_specs=(VM,) * (1 + n_out),
        scratch_shapes=[
            pltpu.VMEM((col_own * len(sources), edge, cols), BF16),
            pltpu.VMEM((strips, tpi, edge, edge), BF16),
            pltpu.SemaphoreType.DMA((strips + 1,)),
        ],
        compiler_params=params(16),
        cost_estimate=cost(strips // 4 if far_only else strips),
        name="sketch_far" if far_only else "sketch_rest",
    )(*scalars, far_off(tiles), far_off(sources[0]),
      *[near(s) for s in (*sources[1:], *after)])


def first_kernel(blocks, piece, mine_ref, pair_ref, out_ref):
    rows = pl.ds(piece * blocks, blocks)
    out_ref[...] = (mine_ref[rows] + pair_ref[rows].astype(F32)).astype(BF16)


def relay_kernel(t, chips, blocks, piece, ints_ref, far_mine, far_pair, rest_mine,
                 rest_pair, even_in, odd_in, even_out, odd_out):
    chip = ints_ref[ME] // 2
    far = far_chip(chip, chips)
    for parity in (0, 1):
        one_way = (chips - t + chip, chip > 0, (odd_in, even_in)[parity],
                   (even_out, odd_out)[parity])
        other_way = (t - chips + chip, chip < chips - 1, (even_in, odd_in)[parity],
                     (odd_out, even_out)[parity])
        for unit, fed, carried, out in (one_way, other_way):
            unit = jnp.clip(unit, 0, chips - 1)

            @pl.when((chip % 2 == parity) & (unit == far))
            def _():
                rows = pl.ds(piece * blocks, blocks)
                more = jnp.where(fed, carried[...].astype(F32), 0.0)
                out[...] = (far_mine[rows] + far_pair[rows].astype(F32) + more).astype(BF16)

            @pl.when((chip % 2 == parity) & (unit != far))
            def _():
                unit_at = unit - (far == 0).astype(jnp.int32)
                rows = pl.ds((piece * (chips - 1) + unit_at) * blocks, blocks)
                there = pl.ds(unit_at * blocks, blocks)
                more = jnp.where(fed, carried[...].astype(F32), 0.0)
                out[...] = (rest_mine[rows] + rest_pair[there].astype(F32) + more).astype(BF16)


def combine_kernel(chips, piece, ints_ref, rest_mine, rest_pair, even_ref,
                   odd_ref, idf_ref, gram_in, sketch_ref, weight_ref, gram_ref):
    blocks = sketch_ref.shape[0]
    chip = ints_ref[ME] // 2
    unit_at = chip - (far_chip(chip, chips) == 0).astype(jnp.int32)
    inner = (chip > 0) & (chip < chips - 1)
    gram = gram_in[...]
    for b in range(blocks):
        at = unit_at * blocks + b
        total = (rest_mine[piece * (chips - 1) * blocks + at] + rest_pair[at].astype(F32) + even_ref[b].astype(F32)
                 + jnp.where(inner, odd_ref[b].astype(F32), 0.0))
        row = idf_ref[pl.ds(piece * blocks + b, 1), :]
        scale = jnp.transpose(jnp.broadcast_to(row, total.shape[::-1]))
        sk = total * scale
        sketch_ref[b] = sk
        weight_ref[b] = jnp.transpose(sk * scale).astype(BF16)
        gram += lax.dot_general(sk, sk, (((0,), (0,)), ((), ())), precision=HIGHEST,
                                preferred_element_type=F32)
    gram_ref[...] = gram


def factor_kernel(total_terms, begin, end, *refs):
    x_ref = refs[-1]
    n = x_ref.shape[0]
    if begin == 0:
        x_ref[...] = refs[0][...] * (1.0 / total_terms)
    else:
        x_ref[...] = refs[0][...]
    rows = lax.broadcasted_iota(jnp.int32, (n, n), 0)
    columns = lax.broadcasted_iota(jnp.int32, (n, n), 1)

    lane = lax.broadcasted_iota(jnp.int32, (8, n), 1)

    def pick(values, at):
        return jnp.take_along_axis(values, jnp.full(values.shape, at, jnp.int32), axis=1)

    def eliminate(trip, carry):
        j = trip * WIDE
        x = x_ref[...]
        row = [jnp.broadcast_to(x_ref[pl.ds(j + k, 1), :], (8, n)) for k in range(WIDE)]
        column = [pick(x, j + k) for k in range(WIDE)]
        block = [[pick(row[k], j + m) for m in range(WIDE)] for k in range(WIDE)]
        scaled = []
        for k in range(WIDE):
            here = lane == j + k
            inverse = 1.0 / block[k][k]
            scaled.append(jnp.where(here, 1.0, row[k]) * inverse)
            for m in range(k + 1, WIDE):
                entry, across = block[m][k], block[k][m] * inverse
                for i in range(k + 1, WIDE):
                    block[m][i] = block[m][i] - entry * (block[k][i] * inverse)
                row[m] = jnp.where(here, 0.0, row[m]) - entry * scaled[k]
                column[m] = column[m] - column[k] * across[:1]
        below = rows >= j + WIDE
        x = jnp.where((columns >= j) & (columns < j + WIDE) & below, 0.0, x)
        for k in range(WIDE):
            passed = (lane > j + k) & (lane < j + WIDE)
            step = jnp.where(passed, 0.0, scaled[k])[:1]
            x = x - jnp.where(below, column[k], 0.0) * step
        x_ref[...] = x
        for k in range(WIDE):
            x_ref[pl.ds(j + k, 1), :] = row[k][:1]
        return carry

    lax.fori_loop(begin // WIDE, end // WIDE, eliminate, jnp.int32(0))
    if end == n:
        x = x_ref[...]
        pivots = jnp.sum(jnp.where(rows == columns, x, 0.0), axis=1, keepdims=True)
        lower = jnp.where(rows > columns, x, jnp.where(rows == columns, 1.0, 0.0))
        x_ref[...] = lower * lax.rsqrt(pivots)


def basis_kernel(inverse_ref, *rest):
    pieces, q_ref = rest[:-1], rest[-1]
    at = 0
    for piece in pieces:
        for b in range(piece.shape[0]):
            q_ref[at] = lax.dot_general(piece[b], inverse_ref[...], (((1,), (1,)), ((), ())),
                                        precision=HIGH, preferred_element_type=F32)
            at += 1


def project_kernel(own_class, chips, owned, away, ints_ref, lists_ref, tiles_ref, *rest):
    sources, rest = rest[:len(away)], rest[len(away):]
    last = own_class == 2
    n_more = 1 if own_class else 0
    before, outs = rest[:n_more], rest[n_more:-4]
    doc_ref, weights_ref, buf_ref, sems = rest[-4:]
    strips, tpi, edge = buf_ref.shape[:3]
    ints = Ints(ints_ref, strips, tpi)
    chip, core = ints.me() // 2, ints.me() % 2
    picked = Picked(lists_ref, strips, 2 + own_class)
    picked.fetch(tiles_ref, buf_ref, sems)
    doc_ref[...] = before[0][...] if n_more else jnp.zeros_like(doc_ref)
    for source, (hops, other, piece) in zip(sources, away):
        there = chip + jnp.where(chip % 2 == 0, hops, -hops)
        size = source.shape[0]

        @pl.when((there >= 0) & (there < chips))
        def _():
            owner = there * 2 + (core if other == 0 else 1 - core)
            weights_ref[pl.ds(owner * owned + piece * size, size)] = source[...]

    def work(strip, at, valid):
        left = weights_ref[ints.group(strip) * owned + ints.slot(strip)]
        right = jnp.concatenate([buf_ref[at, j] for j in range(tpi)], axis=1)
        out = jnp.dot(left, right, preferred_element_type=F32) * valid
        for j in range(tpi):
            doc_ref[ints.column(strip, j)] += out[:, j * edge:(j + 1) * edge]

    picked.in_batches(tiles_ref, buf_ref, sems, work)
    if not last:
        outs[0][...] = doc_ref[...]
    else:
        n_dev, held = len(outs), outs[0].shape[0]
        for s in range(n_dev):
            at = partner_of(n_dev, ints.band(), s) * held
            outs[s][...] = doc_ref[pl.ds(at, held)].astype(outs[s].dtype)


def project(own_class, scalars, tiles, sources, away, before, chips, owned, n_dev, held):
    strips, tpi, edge, _ = tiles.shape
    cols = sources[0].shape[1]
    last = own_class == 2
    if last:
        out_shape = [pltpu.VMEM((held, cols, edge), BF16 if s else F32) for s in range(n_dev)]
    else:
        out_shape = [pltpu.VMEM((n_dev * held, cols, edge), F32)]
    more = [near(before)] if own_class else []
    return pl.pallas_call(
        functools.partial(project_kernel, own_class, chips, owned, away),
        out_shape=out_shape,
        in_specs=[SM] * 2 + [HB] + [VM] * (len(sources) + len(more)),
        out_specs=[VM] * len(out_shape),
        scratch_shapes=[
            pltpu.VMEM((n_dev * held, cols, edge), F32),
            pltpu.VMEM((2 * chips * owned, cols, edge), BF16),
            pltpu.VMEM((strips, tpi, edge, edge), BF16),
            pltpu.SemaphoreType.DMA((strips,)),
        ],
        compiler_params=params(28),
        cost_estimate=cost(strips // 3),
    )(*scalars, far_off(tiles), *[near(s) for s in sources], *more)


def finish_kernel(inverse_ref, own_ref, *rest):
    arrived, out_ref = rest[:-1], rest[-1]
    blocks, _, edge = own_ref.shape
    for b in range(blocks):
        total = own_ref[b]
        for r in arrived:
            total += r[b].astype(F32)
        out_ref[:, b * edge:(b + 1) * edge] = jnp.dot(
            inverse_ref[...], total, precision=HIGHEST, preferred_element_type=F32).astype(BF16)


def on_chip(kernel, out_shape, *args, in_specs=None, scratch=(), mib=8):
    specs = in_specs or [VM] * len(args)
    return pl.pallas_call(
        kernel, out_shape=out_shape, in_specs=specs,
        out_specs=jax.tree.map(lambda _: VM, out_shape,
                               is_leaf=lambda x: not isinstance(x, (tuple, list))),
        scratch_shapes=list(scratch), compiler_params=params(mib),
    )(*[near(a) if s is VM else a for a, s in zip(args, specs)])


def partner_of(n, me, s, back=False):
    if n & (n - 1) == 0:
        return me ^ s
    return (me + (n - s if back else s)) % n


def partners(n, s):
    return [(i, partner_of(n, i, s)) for i in range(n)]


def exchanges(x, axis, n, least=1):
    s, terms = least, [x]
    while s < n:
        x = functools.reduce(jnp.add, terms)
        width = min(4, n // s)
        span = s * width
        terms = [x] + [lax.ppermute(x, axis, [(i, i // span * span + (i + k * s) % span)
                                              for i in range(n)]) for k in range(1, width)]
        s = span
    return terms


def on_device(tiles, tile_col, strip_group, strip_slot, live_count, omega, idf):
    n_group = lax.axis_size("group")
    n_dev = lax.axis_size("dev")
    chips = n_group // 2
    edge = tiles.shape[2]
    cols = omega.shape[1]
    owned = idf.shape[0] // edge
    pieces = PIECES
    blocks = owned // pieces
    me, band = lax.axis_index("group"), lax.axis_index("dev")
    strips, tpi = tile_col.shape
    ints = jnp.concatenate([me[None], band[None], live_count, strip_group, strip_slot]
                           + [tile_col[:, j] for j in range(tpi)]).astype(jnp.int32)
    ints = far_off(ints)

    ints, lists = pl.pallas_call(
        functools.partial(lists_kernel, strips, tpi, chips),
        out_shape=(pltpu.SMEM(ints.shape, jnp.int32),
                   pltpu.SMEM((CLASSES * (strips + 1),), jnp.int32)),
        in_specs=[HB], out_specs=(SM, SM), scratch_shapes=[pltpu.SemaphoreType.DMA],
        compiler_params=params(1), name="lists")(ints)
    ints = pltpu.with_memory_space_constraint(ints, pltpu.SMEM)
    lists = pltpu.with_memory_space_constraint(lists, pltpu.SMEM)
    scalars = (ints, lists)
    swap_links = [(i, i ^ 1) for i in range(n_group)]

    def swap(x):
        return lax.ppermute(x, "group", swap_links)

    even_links = [(2 * c + k, 2 * (c ^ 1) + k) for c in range(chips) for k in (0, 1)]
    odd_links = []
    for c in range(chips):
        to = c + 1 if c % 2 else c - 1
        for k in (0, 1):
            odd_links.append((2 * c + k, 2 * to + k if 0 <= to < chips else 2 * c + 1 - k))

    def over(x, links):
        return lax.ppermute(x, "group", links)

    col_own = omega.shape[0] // edge
    own_omega = omega.reshape(col_own, edge, cols)
    omegas = [own_omega] + [lax.ppermute(own_omega, "dev", partners(n_dev, s))
                            for s in range(1, n_dev)]

    far_mine, far_theirs = partial_sketch(True, scalars, tiles, omegas, chips, blocks)
    far_pair = swap(far_theirs)
    piece_shape = pltpu.VMEM((blocks, edge, cols), BF16)
    first = [on_chip(functools.partial(first_kernel, blocks, p), piece_shape,
                     far_mine, far_pair) for p in range(pieces)]
    evens = [over(x, even_links) for x in first]
    odds = list(evens)
    rest_mine, *rest_theirs = partial_sketch(False, scalars, tiles, omegas, chips, blocks,
                                             first)
    rest_pairs = [swap(x) for x in rest_theirs]
    for t in range(2, chips):
        for p in range(pieces):
            to_even, to_odd = on_chip(
                functools.partial(relay_kernel, t, chips, blocks, p),
                (piece_shape, piece_shape), ints, far_mine, far_pair, rest_mine,
                rest_pairs[p], evens[p], odds[p], in_specs=[SM] + [VM] * 6)
            evens[p] = over(to_even, even_links)
            odds[p] = over(to_odd, odd_links)

    gram = jnp.zeros((cols, cols), F32)
    sketches, weights = [], []
    for p in range(pieces):
        sk, w, gram = on_chip(
            functools.partial(combine_kernel, chips, p),
            (pltpu.VMEM((blocks, edge, cols), F32), pltpu.VMEM((blocks, cols, edge), BF16),
             pltpu.VMEM((cols, cols), F32)),
            ints, rest_mine, rest_pairs[p], evens[p], odds[p],
            idf.reshape(owned, edge), gram, in_specs=[SM] + [VM] * 6)
        sketches.append(sk)
        weights.append(w)

    evens, odds = list(weights), list(weights)
    sources, away = [], []
    for p in range(pieces):
        sources += [weights[p], swap(weights[p])]
        away += [(0, 0, p), (0, 1, p)]
    stages = []
    for t in range(1, chips):
        if t in (2, chips - 1):
            stages.append((sources, away))
            sources, away = [], []
        for p in range(pieces):
            to_even, to_odd = odds[p], evens[p]
            evens[p] = over(to_even, even_links)
            sources += [evens[p], swap(evens[p])]
            away += [(t, 0, p), (t, 1, p)]
            if t < chips - 1:
                odds[p] = over(to_odd, odd_links)
                sources += [odds[p], swap(odds[p])]
                away += [(-t, 0, p), (-t, 1, p)]
    stages.append((sources, away))

    step = 2
    while step < n_group:
        gram = gram + lax.ppermute(gram, "group", partners(n_group, step))
        step *= 2
    gram = functools.reduce(jnp.add, exchanges(gram, "dev", n_dev))
    gram = gram + swap(gram)
    square = pltpu.VMEM((cols, cols), F32)
    total = idf.shape[0] * n_group * n_dev
    inverse = on_chip(functools.partial(factor_kernel, total, 0, cols // 2), square,
                      gram)
    inverse = on_chip(functools.partial(factor_kernel, total, cols // 2, cols), square,
                      inverse)
    q_basis = on_chip(basis_kernel, jax.ShapeDtypeStruct((owned, edge, cols), F32),
                      inverse, *sketches).reshape(owned * edge, cols)

    docs = None
    for own_class, (sources, away) in enumerate(stages):
        docs = project(own_class, scalars, tiles, sources, away, docs, chips, owned, n_dev,
                       col_own)
        docs = docs if own_class == 2 else docs[0]
    parts = docs
    arrived = [lax.ppermute(parts[s], "dev", partners(n_dev, s)) for s in range(1, n_dev)]
    doc_factor = on_chip(finish_kernel, jax.ShapeDtypeStruct((cols, col_own * edge), BF16),
                         inverse, parts[0], *arrived)
    return (q_basis, doc_factor)


def solution(mesh):
    placed = (
        P(("group", "dev"), None, None, None),
        P(("group", "dev"), None),
        P(("group", "dev")),
        P(("group", "dev")),
        P(("group", "dev")),
        P(("group", "dev"), None),
        P(("group", "dev")),
    )

    return jax.shard_map(
        on_device,
        mesh=mesh,
        in_specs=placed,
        out_specs=(P(("group", "dev"), None), P(None, ("group", "dev"))),
        check_vma=False,
    )
```

```python
import functools
import jax
import jax.numpy as jnp
from jax import lax
from jax.experimental import pallas as pl
from jax.experimental.pallas import tpu as pltpu
from jax.sharding import PartitionSpec as P

F32 = jnp.float32
BF16 = jnp.bfloat16
HIGH = lax.Precision.HIGH
HIGHEST = lax.Precision.HIGHEST
BATCH = 4
WIDE = 4
PIECES = 2

VM = pl.BlockSpec(memory_space=pltpu.VMEM)
SM = pl.BlockSpec(memory_space=pltpu.SMEM)
HB = pl.BlockSpec(memory_space=pltpu.HBM)


def near(x):
    return pltpu.with_memory_space_constraint(x, pltpu.VMEM)


def far_off(x):
    return pltpu.with_memory_space_constraint(x, pltpu.HBM)


def cost(strips):
    return pl.CostEstimate(flops=strips << 28, bytes_accessed=strips << 19, transcendentals=0)


def params(mib):
    return pltpu.CompilerParams(vmem_limit_bytes=mib << 20)


ME, BAND, LIVE, LISTS = 0, 1, 2, 3


class Ints:
    def __init__(self, ref, strips, tpi):
        self.ref, self.strips, self.tpi = ref, strips, tpi

    def me(self):
        return self.ref[ME]

    def band(self):
        return self.ref[BAND]

    def live(self):
        return self.ref[LIVE]

    def group(self, strip):
        return self.ref[LISTS + strip]

    def slot(self, strip):
        return self.ref[LISTS + self.strips + strip]

    def column(self, strip, j):
        return self.ref[LISTS + (2 + j) * self.strips + strip]


def far_chip(chip, chips):
    return jnp.where(chip < chips // 2, chips - 1, 0)


CLASSES = 5


def lists_kernel(strips, tpi, chips, given_ref, ints_ref, lists_ref, sem):
    copy = pltpu.make_async_copy(given_ref, ints_ref, sem)
    copy.start()
    copy.wait()
    ints = Ints(ints_ref, strips, tpi)
    chip = ints.me() // 2
    far = far_chip(chip, chips)

    def scan(strip, counts):
        owner = ints.group(strip) // 2
        hops = abs(owner - chip)
        is_far, is_last, is_near = owner == far, hops == chips - 1, hops <= 1
        n_far, n_near, n_last = counts
        n_mid = strip - n_near - n_last
        lists_ref[jnp.where(is_far, n_far, strips + strip - n_far)] = strip
        lists_ref[jnp.where(is_near, 2 * strips + n_near,
                            jnp.where(is_last, 4 * strips + n_last, 3 * strips + n_mid))] = strip
        return tuple(n + hit.astype(jnp.int32)
                     for n, hit in zip(counts, (is_far, is_near, is_last)))

    n_far, n_near, n_last = lax.fori_loop(0, ints.live(), scan, (jnp.int32(0),) * 3)
    n_all = ints.live()
    for c, count in enumerate((n_far, n_all - n_far, n_near, n_all - n_near - n_last, n_last)):
        lists_ref[CLASSES * strips + c] = count


class Picked:
    def __init__(self, lists_ref, strips, own):
        self.lists, self.start = lists_ref, own * strips
        self.count = lists_ref[CLASSES * strips + own]

    def strip(self, at):
        return self.lists[self.start + at]

    def fetch(self, tiles_ref, buf_ref, sems):
        def begin(at, carry):
            pltpu.make_async_copy(tiles_ref.at[self.strip(at)], buf_ref.at[at],
                                  sems.at[at]).start()
            return carry

        lax.fori_loop(0, self.count, begin, jnp.int32(0))

    def in_batches(self, tiles_ref, buf_ref, sems, work, batch=BATCH):
        def trip(b, carry):
            for i in range(batch):
                at = b * batch + i

                @pl.when(at < self.count)
                def _():
                    pltpu.make_async_copy(tiles_ref.at[0], buf_ref.at[at], sems.at[at]).wait()

            for i in range(batch):
                at = jnp.minimum(b * batch + i, self.count - 1)
                work(self.strip(at), at, (b * batch + i < self.count).astype(F32))
            return carry

        lax.fori_loop(0, (self.count + batch - 1) // batch, trip, jnp.int32(0))


def sketch_kernel(far_only, chips, blocks, n_src, ints_ref, lists_ref, tiles_ref, *rest):
    sources = rest[:n_src]
    both_ref, *theirs, omega_ref, buf_ref, sems = rest[-3 - 1 - (1 if far_only else PIECES):]
    half = both_ref.shape[0] // 2
    units = half // (PIECES * blocks)
    strips, tpi = buf_ref.shape[:2]
    ints = Ints(ints_ref, strips, tpi)
    chip, core, band = ints.me() // 2, ints.me() % 2, ints.band()
    far = far_chip(chip, chips)
    held = sources[0].shape[0]
    own = pltpu.make_async_copy(sources[0], omega_ref.at[pl.ds(band * held, held)],
                                sems.at[strips])
    own.start()
    picked = Picked(lists_ref, strips, 0 if far_only else 1)
    picked.fetch(tiles_ref, buf_ref, sems)
    both_ref[...] = jnp.zeros_like(both_ref)
    for s in range(1, n_src):
        omega_ref[pl.ds(partner_of(n_src, band, s, back=True) * held, held)] = sources[s][...]
    own.wait()

    def work(strip, at, valid):
        owner = ints.group(strip)
        unit = jnp.int32(0) if far_only else owner // 2 - (far == 0).astype(jnp.int32)
        side = jnp.where(owner % 2 == core, 0, half)
        piece, slot = ints.slot(strip) // blocks, ints.slot(strip) % blocks
        block = side + (piece * units + unit) * blocks + slot
        left = jnp.concatenate([buf_ref[at, j] for j in range(tpi)], axis=1)
        right = jnp.concatenate([omega_ref[ints.column(strip, j)] for j in range(tpi)], axis=0)
        both_ref[block] += jnp.dot(left, right, preferred_element_type=F32) * valid

    picked.in_batches(tiles_ref, buf_ref, sems, work, BATCH if far_only else 2 * BATCH)
    size = half // len(theirs)
    for p, out in enumerate(theirs):
        out[...] = both_ref[pl.ds(half + p * size, size)].astype(BF16)


def partial_sketch(far_only, scalars, tiles, sources, chips, blocks, after=()):
    strips, tpi, edge, _ = tiles.shape
    col_own, _, cols = sources[0].shape
    half = PIECES * blocks * (1 if far_only else chips - 1)
    n_out = 1 if far_only else PIECES
    return pl.pallas_call(
        functools.partial(sketch_kernel, far_only, chips, blocks, len(sources)),
        out_shape=(pltpu.VMEM((2 * half, edge, cols), F32),)
        + (pltpu.VMEM((half // n_out, edge, cols), BF16),) * n_out,
        in_specs=[SM] * 2 + [HB] * 2 + [VM] * (len(sources) - 1 + len(after)),
        out_specs=(VM,) * (1 + n_out),
        scratch_shapes=[
            pltpu.VMEM((col_own * len(sources), edge, cols), BF16),
            pltpu.VMEM((strips, tpi, edge, edge), BF16),
            pltpu.SemaphoreType.DMA((strips + 1,)),
        ],
        compiler_params=params(16),
        cost_estimate=cost(strips // 4 if far_only else strips),
        name="sketch_far" if far_only else "sketch_rest",
    )(*scalars, far_off(tiles), far_off(sources[0]),
      *[near(s) for s in (*sources[1:], *after)])


def first_kernel(blocks, piece, mine_ref, pair_ref, out_ref):
    rows = pl.ds(piece * blocks, blocks)
    out_ref[...] = (mine_ref[rows] + pair_ref[rows].astype(F32)).astype(BF16)


def relay_kernel(t, chips, blocks, piece, ints_ref, far_mine, far_pair, rest_mine,
                 rest_pair, even_in, odd_in, even_out, odd_out):
    chip = ints_ref[ME] // 2
    far = far_chip(chip, chips)
    for parity in (0, 1):
        one_way = (chips - t + chip, chip > 0, (odd_in, even_in)[parity],
                   (even_out, odd_out)[parity])
        other_way = (t - chips + chip, chip < chips - 1, (even_in, odd_in)[parity],
                     (odd_out, even_out)[parity])
        for unit, fed, carried, out in (one_way, other_way):
            unit = jnp.clip(unit, 0, chips - 1)

            @pl.when((chip % 2 == parity) & (unit == far))
            def _():
                rows = pl.ds(piece * blocks, blocks)
                more = jnp.where(fed, carried[...].astype(F32), 0.0)
                out[...] = (far_mine[rows] + far_pair[rows].astype(F32) + more).astype(BF16)

            @pl.when((chip % 2 == parity) & (unit != far))
            def _():
                unit_at = unit - (far == 0).astype(jnp.int32)
                rows = pl.ds((piece * (chips - 1) + unit_at) * blocks, blocks)
                there = pl.ds(unit_at * blocks, blocks)
                more = jnp.where(fed, carried[...].astype(F32), 0.0)
                out[...] = (rest_mine[rows] + rest_pair[there].astype(F32) + more).astype(BF16)


def combine_kernel(chips, piece, ints_ref, rest_mine, rest_pair, even_ref,
                   odd_ref, idf_ref, gram_in, sketch_ref, weight_ref, gram_ref):
    blocks = sketch_ref.shape[0]
    chip = ints_ref[ME] // 2
    unit_at = chip - (far_chip(chip, chips) == 0).astype(jnp.int32)
    inner = (chip > 0) & (chip < chips - 1)
    gram = gram_in[...]
    for b in range(blocks):
        at = unit_at * blocks + b
        total = (rest_mine[piece * (chips - 1) * blocks + at] + rest_pair[at].astype(F32) + even_ref[b].astype(F32)
                 + jnp.where(inner, odd_ref[b].astype(F32), 0.0))
        row = idf_ref[pl.ds(piece * blocks + b, 1), :]
        scale = jnp.transpose(jnp.broadcast_to(row, total.shape[::-1]))
        sk = total * scale
        sketch_ref[b] = sk
        weight_ref[b] = jnp.transpose(sk * scale).astype(BF16)
        gram += lax.dot_general(sk, sk, (((0,), (0,)), ((), ())), precision=HIGHEST,
                                preferred_element_type=F32)
    gram_ref[...] = gram


def factor_kernel(total_terms, begin, end, *refs):
    x_ref = refs[-1]
    n = x_ref.shape[0]
    if begin == 0:
        x_ref[...] = refs[0][...] * (1.0 / total_terms)
    else:
        x_ref[...] = refs[0][...]
    rows = lax.broadcasted_iota(jnp.int32, (n, n), 0)
    columns = lax.broadcasted_iota(jnp.int32, (n, n), 1)

    lane = lax.broadcasted_iota(jnp.int32, (8, n), 1)

    def pick(values, at):
        return jnp.take_along_axis(values, jnp.full(values.shape, at, jnp.int32), axis=1)

    def eliminate(trip, carry):
        j = trip * WIDE
        x = x_ref[...]
        row = [jnp.broadcast_to(x_ref[pl.ds(j + k, 1), :], (8, n)) for k in range(WIDE)]
        column = [pick(x, j + k) for k in range(WIDE)]
        block = [[pick(row[k], j + m) for m in range(WIDE)] for k in range(WIDE)]
        scaled = []
        for k in range(WIDE):
            here = lane == j + k
            inverse = 1.0 / block[k][k]
            scaled.append(jnp.where(here, 1.0, row[k]) * inverse)
            for m in range(k + 1, WIDE):
                entry, across = block[m][k], block[k][m] * inverse
                for i in range(k + 1, WIDE):
                    block[m][i] = block[m][i] - entry * (block[k][i] * inverse)
                row[m] = jnp.where(here, 0.0, row[m]) - entry * scaled[k]
                column[m] = column[m] - column[k] * across[:1]
        below = rows >= j + WIDE
        x = jnp.where((columns >= j) & (columns < j + WIDE) & below, 0.0, x)
        for k in range(WIDE):
            passed = (lane > j + k) & (lane < j + WIDE)
            step = jnp.where(passed, 0.0, scaled[k])[:1]
            x = x - jnp.where(below, column[k], 0.0) * step
        x_ref[...] = x
        for k in range(WIDE):
            x_ref[pl.ds(j + k, 1), :] = row[k][:1]
        return carry

    lax.fori_loop(begin // WIDE, end // WIDE, eliminate, jnp.int32(0))
    if end == n:
        x = x_ref[...]
        pivots = jnp.sum(jnp.where(rows == columns, x, 0.0), axis=1, keepdims=True)
        lower = jnp.where(rows > columns, x, jnp.where(rows == columns, 1.0, 0.0))
        x_ref[...] = lower * lax.rsqrt(pivots)


def basis_kernel(inverse_ref, *rest):
    pieces, q_ref = rest[:-1], rest[-1]
    at = 0
    for piece in pieces:
        for b in range(piece.shape[0]):
            q_ref[at] = lax.dot_general(piece[b], inverse_ref[...], (((1,), (1,)), ((), ())),
                                        precision=HIGH, preferred_element_type=F32)
            at += 1


def project_kernel(own_class, chips, owned, away, ints_ref, lists_ref, tiles_ref, *rest):
    sources, rest = rest[:len(away)], rest[len(away):]
    last = own_class == 2
    n_more = 1 if own_class else 0
    before, outs = rest[:n_more], rest[n_more:-4]
    doc_ref, weights_ref, buf_ref, sems = rest[-4:]
    strips, tpi, edge = buf_ref.shape[:3]
    ints = Ints(ints_ref, strips, tpi)
    chip, core = ints.me() // 2, ints.me() % 2
    picked = Picked(lists_ref, strips, 2 + own_class)
    picked.fetch(tiles_ref, buf_ref, sems)
    doc_ref[...] = before[0][...] if n_more else jnp.zeros_like(doc_ref)
    for source, (hops, other, piece) in zip(sources, away):
        there = chip + jnp.where(chip % 2 == 0, hops, -hops)
        size = source.shape[0]

        @pl.when((there >= 0) & (there < chips))
        def _():
            owner = there * 2 + (core if other == 0 else 1 - core)
            weights_ref[pl.ds(owner * owned + piece * size, size)] = source[...]

    def work(strip, at, valid):
        left = weights_ref[ints.group(strip) * owned + ints.slot(strip)]
        right = jnp.concatenate([buf_ref[at, j] for j in range(tpi)], axis=1)
        out = jnp.dot(left, right, preferred_element_type=F32) * valid
        for j in range(tpi):
            doc_ref[ints.column(strip, j)] += out[:, j * edge:(j + 1) * edge]

    picked.in_batches(tiles_ref, buf_ref, sems, work)
    if not last:
        outs[0][...] = doc_ref[...]
    else:
        n_dev, held = len(outs), outs[0].shape[0]
        for s in range(n_dev):
            at = partner_of(n_dev, ints.band(), s) * held
            outs[s][...] = doc_ref[pl.ds(at, held)].astype(outs[s].dtype)


def project(own_class, scalars, tiles, sources, away, before, chips, owned, n_dev, held):
    strips, tpi, edge, _ = tiles.shape
    cols = sources[0].shape[1]
    last = own_class == 2
    if last:
        out_shape = [pltpu.VMEM((held, cols, edge), BF16 if s else F32) for s in range(n_dev)]
    else:
        out_shape = [pltpu.VMEM((n_dev * held, cols, edge), F32)]
    more = [near(before)] if own_class else []
    return pl.pallas_call(
        functools.partial(project_kernel, own_class, chips, owned, away),
        out_shape=out_shape,
        in_specs=[SM] * 2 + [HB] + [VM] * (len(sources) + len(more)),
        out_specs=[VM] * len(out_shape),
        scratch_shapes=[
            pltpu.VMEM((n_dev * held, cols, edge), F32),
            pltpu.VMEM((2 * chips * owned, cols, edge), BF16),
            pltpu.VMEM((strips, tpi, edge, edge), BF16),
            pltpu.SemaphoreType.DMA((strips,)),
        ],
        compiler_params=params(28),
        cost_estimate=cost(strips // 3),
    )(*scalars, far_off(tiles), *[near(s) for s in sources], *more)


def finish_kernel(inverse_ref, own_ref, *rest):
    arrived, out_ref = rest[:-1], rest[-1]
    blocks, _, edge = own_ref.shape
    for b in range(blocks):
        total = own_ref[b]
        for r in arrived:
            total += r[b].astype(F32)
        out_ref[:, b * edge:(b + 1) * edge] = jnp.dot(
            inverse_ref[...], total, precision=HIGHEST, preferred_element_type=F32).astype(BF16)


def on_chip(kernel, out_shape, *args, in_specs=None, scratch=(), mib=8):
    specs = in_specs or [VM] * len(args)
    return pl.pallas_call(
        kernel, out_shape=out_shape, in_specs=specs,
        out_specs=jax.tree.map(lambda _: VM, out_shape,
                               is_leaf=lambda x: not isinstance(x, (tuple, list))),
        scratch_shapes=list(scratch), compiler_params=params(mib),
    )(*[near(a) if s is VM else a for a, s in zip(args, specs)])


def partner_of(n, me, s, back=False):
    if n & (n - 1) == 0:
        return me ^ s
    return (me + (n - s if back else s)) % n


def partners(n, s):
    return [(i, partner_of(n, i, s)) for i in range(n)]


def exchanges(x, axis, n, least=1):
    s, terms = least, [x]
    while s < n:
        x = functools.reduce(jnp.add, terms)
        width = min(4, n // s)
        span = s * width
        terms = [x] + [lax.ppermute(x, axis, [(i, i // span * span + (i + k * s) % span)
                                              for i in range(n)]) for k in range(1, width)]
        s = span
    return terms


def on_device(tiles, tile_col, strip_group, strip_slot, live_count, omega, idf):
    n_group = lax.axis_size("group")
    n_dev = lax.axis_size("dev")
    chips = n_group // 2
    edge = tiles.shape[2]
    cols = omega.shape[1]
    owned = idf.shape[0] // edge
    pieces = PIECES
    blocks = owned // pieces
    me, band = lax.axis_index("group"), lax.axis_index("dev")
    strips, tpi = tile_col.shape
    ints = jnp.concatenate([me[None], band[None], live_count, strip_group, strip_slot]
                           + [tile_col[:, j] for j in range(tpi)]).astype(jnp.int32)
    ints = far_off(ints)

    ints, lists = pl.pallas_call(
        functools.partial(lists_kernel, strips, tpi, chips),
        out_shape=(pltpu.SMEM(ints.shape, jnp.int32),
                   pltpu.SMEM((CLASSES * (strips + 1),), jnp.int32)),
        in_specs=[HB], out_specs=(SM, SM), scratch_shapes=[pltpu.SemaphoreType.DMA],
        compiler_params=params(1), name="lists")(ints)
    ints = pltpu.with_memory_space_constraint(ints, pltpu.SMEM)
    lists = pltpu.with_memory_space_constraint(lists, pltpu.SMEM)
    scalars = (ints, lists)
    swap_links = [(i, i ^ 1) for i in range(n_group)]

    def swap(x):
        return lax.ppermute(x, "group", swap_links)

    even_links = [(2 * c + k, 2 * (c ^ 1) + k) for c in range(chips) for k in (0, 1)]
    odd_links = []
    for c in range(chips):
        to = c + 1 if c % 2 else c - 1
        for k in (0, 1):
            odd_links.append((2 * c + k, 2 * to + k if 0 <= to < chips else 2 * c + 1 - k))

    def over(x, links):
        return lax.ppermute(x, "group", links)

    col_own = omega.shape[0] // edge
    own_omega = omega.reshape(col_own, edge, cols)

    def to_dev(x, k):
        return lax.ppermute(x, "dev", partners(n_dev, k))

    omegas = [own_omega] + [to_dev(own_omega, k) for k in range(1, n_dev)]

    far_mine, far_theirs = partial_sketch(True, scalars, tiles, omegas, chips, blocks)
    far_pair = swap(far_theirs)
    piece_shape = pltpu.VMEM((blocks, edge, cols), BF16)
    first = [on_chip(functools.partial(first_kernel, blocks, p), piece_shape,
                     far_mine, far_pair) for p in range(pieces)]
    evens = [over(x, even_links) for x in first]
    odds = list(evens)
    rest_mine, *rest_theirs = partial_sketch(False, scalars, tiles, omegas, chips, blocks,
                                             first)
    rest_pairs = [swap(x) for x in rest_theirs]
    for t in range(2, chips):
        for p in range(pieces):
            to_even, to_odd = on_chip(
                functools.partial(relay_kernel, t, chips, blocks, p),
                (piece_shape, piece_shape), ints, far_mine, far_pair, rest_mine,
                rest_pairs[p], evens[p], odds[p], in_specs=[SM] + [VM] * 6)
            evens[p] = over(to_even, even_links)
            odds[p] = over(to_odd, odd_links)

    gram = jnp.zeros((cols, cols), F32)
    sketches, weights = [], []
    for p in range(pieces):
        sk, w, gram = on_chip(
            functools.partial(combine_kernel, chips, p),
            (pltpu.VMEM((blocks, edge, cols), F32), pltpu.VMEM((blocks, cols, edge), BF16),
             pltpu.VMEM((cols, cols), F32)),
            ints, rest_mine, rest_pairs[p], evens[p], odds[p],
            idf.reshape(owned, edge), gram, in_specs=[SM] + [VM] * 6)
        sketches.append(sk)
        weights.append(w)

    evens, odds = list(weights), list(weights)
    sources, away = [], []
    for p in range(pieces):
        sources += [weights[p], swap(weights[p])]
        away += [(0, 0, p), (0, 1, p)]
    stages = []
    for t in range(1, chips):
        if t in (2, chips - 1):
            stages.append((sources, away))
            sources, away = [], []
        for p in range(pieces):
            to_even, to_odd = odds[p], evens[p]
            evens[p] = over(to_even, even_links)
            sources += [evens[p], swap(evens[p])]
            away += [(t, 0, p), (t, 1, p)]
            if t < chips - 1:
                odds[p] = over(to_odd, odd_links)
                sources += [odds[p], swap(odds[p])]
                away += [(-t, 0, p), (-t, 1, p)]
    stages.append((sources, away))

    step = 2
    while step < n_group:
        gram = gram + lax.ppermute(gram, "group", partners(n_group, step))
        step *= 2
    gram = functools.reduce(jnp.add, exchanges(gram, "dev", n_dev))
    gram = gram + swap(gram)
    square = pltpu.VMEM((cols, cols), F32)
    total = idf.shape[0] * n_group * n_dev
    inverse = on_chip(functools.partial(factor_kernel, total, 0, cols // 2), square,
                      gram)
    inverse = on_chip(functools.partial(factor_kernel, total, cols // 2, cols), square,
                      inverse)
    q_basis = on_chip(basis_kernel, jax.ShapeDtypeStruct((owned, edge, cols), F32),
                      inverse, *sketches).reshape(owned * edge, cols)

    docs = None
    for own_class, (sources, away) in enumerate(stages):
        docs = project(own_class, scalars, tiles, sources, away, docs, chips, owned, n_dev,
                       col_own)
        docs = docs if own_class == 2 else docs[0]
    parts = docs
    arrived = [to_dev(parts[k], k) for k in range(1, n_dev)]
    doc_factor = on_chip(finish_kernel, jax.ShapeDtypeStruct((cols, col_own * edge), BF16),
                         inverse, parts[0], *arrived)
    return (q_basis, doc_factor)


def solution(mesh):
    placed = (
        P(("group", "dev"), None, None, None),
        P(("group", "dev"), None),
        P(("group", "dev")),
        P(("group", "dev")),
        P(("group", "dev")),
        P(("group", "dev"), None),
        P(("group", "dev")),
    )

    return jax.shard_map(
        on_device,
        mesh=mesh,
        in_specs=placed,
        out_specs=(P(("group", "dev"), None), P(None, ("group", "dev"))),
        check_vma=False,
    )
```
